32 devices in a mesh: ma: 8 (over z, y), row: 4 (over x, core).
Axes of the slice: x: 2, y: 2, z: 4, core: 2. Of those that a mesh axis runs over, the one named last changes fastest.
Arguments:
- velocity: bfloat16 [3, 2, 16, 32, 65], P(None, None, 'row', 'ma'), may hold values from -6 to 6
- vorticity: bfloat16 [3, 2, 16, 32, 65], P(None, None, 'row', 'ma'), may hold values from -6 to 6
- legendre: bfloat16 [32, 65, 384], P('ma'), may hold values from -0.75 to 0.75
- pair_order: int32 [32], P('ma'), may hold values from 0 to 31, each once
- lat_weight: float32 [384], replicated, may hold values from 0.5 to 2
- diffusivity: float32 [16], replicated, may hold values from 0.25 to 2.5
Outputs:
- new_velocity: float32 [3, 2, 16, 32, 65], P(None, None, 'row', 'ma')
The draws below stay inside these ranges and needn't reach their ends.
Inputs may be any that keep to these rules, and one draw needn't show every extreme that they name: pair_order holds each of 0 to 31 exactly once.
All inputs are finite; a program needn't handle non-finite values.
Results may differ from the reference program's by a relative error of at most 0.0095.
Values may be sent and summed in bfloat16 or wider, within the bound.
A program may use at most 128 MiB of HBM per device.

```python
import math
import jax
import jax.numpy as jnp
from jax import lax

ORDERS = 64
PAIRS = 32
PACK = 65
NLAT = 768
NH = 384
NLON = 2048
LEVELS = 16


def shard_levels(rng, dims, cuts, least, largest):
    def one(position, shards_of):
        heights = jax.random.uniform(jax.random.fold_in(jax.random.fold_in(rng, 6), position), (shards_of,), jnp.float32, least / len(cuts), largest / len(cuts))
        return jnp.repeat(jnp.exp(heights), dims[position] // shards_of).reshape((-1,) + (1,) * (len(dims) - position - 1))

    gain = one(*cuts[0])
    for cut in cuts[1:]:
        gain = gain * one(*cut)
    return gain


def bell_draw(own_key, extent, scale, bound, cuts=(), kind=jnp.bfloat16):
    drawn = jax.random.normal(own_key, extent, jnp.float32) * scale
    if len(cuts) > 0:
        drawn = shard_levels(own_key, extent, cuts, -0.22, 0.18) * drawn
    return jnp.clip(drawn, min=-bound, max=bound).astype(kind)


def setup_inputs(seed: int = 0) -> dict:
    splits = jax.random.split(jax.random.key(seed), 7)
    velocity = bell_draw(splits[0], (3, 2, LEVELS, PAIRS, PACK), 1.0, 6.0, ((2, 4), (3, 8)))
    vorticity = bell_draw(splits[1], (3, 2, LEVELS, PAIRS, PACK), 1.0, 6.0, ((2, 4), (3, 8)))
    legendre = bell_draw(splits[2], (PAIRS, PACK, NH), ORDERS ** -0.5, 0.75, ((0, 8),))
    pair_order = jax.random.permutation(splits[3], PAIRS).astype(jnp.int32)
    lat_weight = jnp.clip(jnp.exp(jax.random.uniform(splits[4], (NH,), jnp.float32, math.log(0.5), math.log(2.0))), 0.5, 2.0)
    diffusivity = jnp.clip(jnp.exp(jax.random.uniform(splits[5], (LEVELS,), jnp.float32, math.log(0.25), math.log(2.5))), 0.25, 2.5)
    return {"velocity": velocity, "vorticity": vorticity, "legendre": legendre, "pair_order": pair_order, "lat_weight": lat_weight, "diffusivity": diffusivity}


STEP_SIZE = 1.0

def row_masks(low_order):
    row_index = jnp.arange(PACK, dtype=jnp.int32)[None, :]
    low_column = low_order[:, None]
    is_lower = row_index < ORDERS - low_column
    not_lower = jnp.logical_not(is_lower)
    even_low = row_index % 2 == 0
    even_high = (row_index + low_column) % 2 == 0
    low_pair = jnp.stack([is_lower & even_low, is_lower & jnp.logical_not(even_low)])
    high_pair = jnp.stack([not_lower & even_high, not_lower & jnp.logical_not(even_high)])
    return jnp.stack([low_pair, high_pair]).astype(jnp.float32)

def cross_product(velocity_grid, vorticity_grid):
    return jnp.stack([velocity_grid[1] * vorticity_grid[2] - velocity_grid[2] * vorticity_grid[1], velocity_grid[2] * vorticity_grid[0] - velocity_grid[0] * vorticity_grid[2], velocity_grid[0] * vorticity_grid[1] - velocity_grid[1] * vorticity_grid[0]])

def synth_pair(packed):
    coeffs, legendre_rows, low_order = packed
    mask_table = row_masks(low_order[None])[:, :, 0]
    masked = coeffs.astype(jnp.float32)[None, None] * mask_table[:, :, None, None, None, :]
    halves = jnp.einsum('oqfilr,rj->qflioj', masked, legendre_rows.astype(jnp.float32))
    north_part = halves[0] + halves[1]
    south_part = halves[0] - halves[1]
    return jnp.concatenate([north_part, south_part], axis=-1).astype(jnp.bfloat16)

def grid_level(spectra):
    values = lax.optimization_barrier(spectra).astype(jnp.float32)
    doubled = jnp.where(jnp.arange(ORDERS) == 0, 2.0, 1.0).astype(values.dtype)
    coefficient = lax.complex(values[:, 0] * doubled, values[:, 1] * doubled)
    coefficient = jnp.pad(coefficient, ((0, 0), (0, 0), (0, NLON // 2 + 1 - ORDERS)))
    fields = jnp.fft.irfft(coefficient, n=NLON, axis=-1) * (NLON / (2.0 * math.sqrt(ORDERS)))
    lamb_vector = cross_product(fields[:3], fields[3:])
    spectrum = jnp.fft.rfft(lamb_vector, axis=-1)[..., :ORDERS] / math.sqrt(NLON)
    return jnp.stack([jnp.real(spectrum), jnp.imag(spectrum)], axis=1).astype(jnp.bfloat16)

def jacobi_sweep(current, source, coupling):
    padded = jnp.pad(current, ((0, 0), (0, 0), (1, 1), (0, 0), (0, 0)))
    return (source + coupling * (padded[:, :, :-2] + padded[:, :, 2:])) / (1.0 + 2.0 * coupling)

def reference(velocity, vorticity, legendre, pair_order, lat_weight, diffusivity):
    fields = jnp.concatenate([velocity, vorticity], axis=0)
    by_pair = jnp.transpose(fields, (3, 0, 1, 2, 4))
    synthesized = lax.map(synth_pair, (by_pair, legendre, pair_order))
    low_part = synthesized[:, :, :, :, 0]
    high_part = synthesized[:, :, :, :, 1]
    by_order = jnp.zeros((ORDERS, 6, LEVELS, 2, NLAT), jnp.bfloat16)
    by_order = by_order.at[pair_order].set(low_part).at[ORDERS - 1 - pair_order].set(high_part)
    by_level = jnp.transpose(by_order, (2, 1, 3, 4, 0))
    lamb_spectra = lax.map(grid_level, by_level)
    lamb_by_order = jnp.transpose(lamb_spectra, (4, 0, 1, 2, 3))

    def analyse_pair(packed):
        legendre_rows, low_order = packed
        mask_table = row_masks(low_order[None])[:, :, 0]
        chosen = jnp.stack([lamb_by_order[low_order], lamb_by_order[ORDERS - 1 - low_order]])
        chosen = lax.optimization_barrier(chosen).astype(jnp.float32)
        north_part = chosen[..., :NH]
        south_part = chosen[..., NH:]
        weighted = jnp.stack([lat_weight * (north_part + south_part), lat_weight * (north_part - south_part)])
        weighted = lax.optimization_barrier(weighted.astype(jnp.bfloat16)).astype(jnp.float32)
        projected = jnp.einsum('qolfij,rj->qolfir', weighted, legendre_rows.astype(jnp.float32))
        selector = jnp.transpose(mask_table, (1, 0, 2))[:, :, None, None, None, :]
        picked = lax.optimization_barrier(jnp.sum(projected * selector, axis=(0, 1)))
        return jnp.transpose(picked, (1, 2, 0, 3))
    tendency = lax.map(analyse_pair, (legendre, pair_order))
    tendency = jnp.transpose(tendency, (1, 2, 3, 0, 4))
    source = velocity.astype(jnp.float32) + STEP_SIZE * tendency
    coupling = diffusivity[None, None, :, None, None]
    first_pass = jacobi_sweep(source, source, coupling)
    return jacobi_sweep(first_pass, source, coupling)
```

```python
import functools
import math

import jax
import jax.numpy as jnp
import numpy as np
from jax import lax
from jax.experimental import pallas as pl
from jax.experimental.pallas import tpu as pltpu
from jax.sharding import PartitionSpec as P

NLON = 2048


STEP_SIZE = 1.0


def with_halo(cells, sides, width):
    for axis, dim in sides:
        count = lax.axis_size(axis)
        ends = count - 1
        head = lax.slice_in_dim(cells, 0, width, axis=dim)
        tail = lax.slice_in_dim(cells, cells.shape[dim] - width, cells.shape[dim], axis=dim)
        cells = jnp.concatenate(
            [
                lax.ppermute(tail, axis, [(i, (i + 1) % count) for i in range(ends)]),
                cells,
                lax.ppermute(head, axis, [((i + 1) % count, i) for i in range(ends)]),
            ],
            axis=dim,
        )
    return cells


def row_masks(low_order, pack_rows):
    orders_all = pack_rows - 1
    row_index = jnp.arange(pack_rows, dtype=jnp.int32)[None, :]
    low_column = low_order[:, None]
    is_lower = row_index < orders_all - low_column
    not_lower = jnp.logical_not(is_lower)
    even_low = row_index % 2 == 0
    even_high = (row_index + low_column) % 2 == 0
    low_pair = jnp.stack([is_lower & even_low, is_lower & jnp.logical_not(even_low)])
    high_pair = jnp.stack([not_lower & even_high, not_lower & jnp.logical_not(even_high)])
    return jnp.stack([low_pair, high_pair])


def cross_product(velocity_grid, vorticity_grid):
    return jnp.stack(
        [
            velocity_grid[1] * vorticity_grid[2] - velocity_grid[2] * vorticity_grid[1],
            velocity_grid[2] * vorticity_grid[0] - velocity_grid[0] * vorticity_grid[2],
            velocity_grid[0] * vorticity_grid[1] - velocity_grid[1] * vorticity_grid[0],
        ]
    )


def lon_table(column_order, is_imag, lon_start, lon_count):
    lon_index = lon_start + jnp.arange(lon_count, dtype=jnp.int32)
    angle_index = column_order[:, None] * lon_index[None, :] % NLON
    angle_value = angle_index.astype(jnp.float32) * (2.0 * math.pi / NLON)
    return jnp.where(is_imag[:, None], -jnp.sin(angle_value), jnp.cos(angle_value))


def local(velocity, vorticity, legendre, pair_order, lat_weight, diffusivity):
    pair_count = pair_order.shape[0]
    pack_rows = legendre.shape[1]
    half_lat = legendre.shape[2]
    nlat_all = 2 * half_lat
    levels_dev = velocity.shape[2]
    orders_all = pack_rows - 1
    inv_orders = 1.0 / math.sqrt(orders_all)
    inv_lon = 1.0 / math.sqrt(NLON)
    lon_width = NLON // 4
    mask_bool = row_masks(pair_order, pack_rows)
    fields = jnp.concatenate([velocity, vorticity], axis=0)
    masked = fields[None, None] * mask_bool.astype(jnp.bfloat16)[:, :, None, None, None]
    halves = jnp.einsum(
        "oqfilsr,srj->qfliosj", masked, legendre, preferred_element_type=jnp.float32
    )
    north_part = halves[0] + halves[1]
    south_part = halves[0] - halves[1]
    both_parts = jnp.concatenate([north_part, south_part], axis=-1)
    spectral = jnp.transpose(both_parts, (0, 1, 5, 2, 3, 4))
    spectral = spectral.reshape(6, levels_dev, nlat_all, 4 * pair_count).astype(jnp.bfloat16)
    gathered_ids = lax.all_gather(pair_order, "ma", axis=0, tiled=True)
    pair_slots = gathered_ids.reshape(-1, 1, 1, pair_count)
    both_orders = jnp.concatenate([pair_slots, orders_all - 1 - pair_slots], axis=2)
    full_shape = (both_orders.shape[0], 2, 2, pair_count)
    column_order = jnp.broadcast_to(both_orders, full_shape).reshape(-1)
    part_index = jnp.arange(2, dtype=jnp.int32)[None, :, None, None]
    is_imag = jnp.broadcast_to(part_index, full_shape).reshape(-1) == 1
    tables = [
        lon_table(column_order, is_imag, lon_block * lon_width, lon_width).astype(jnp.bfloat16)
        for lon_block in range(4)
    ]
    spec_block = lax.all_to_all(spectral, "ma", split_axis=2, concat_axis=3, tiled=True)
    accumulated = jnp.zeros((3,) + spec_block.shape[1:], jnp.float32)
    for lon_block in range(4):
        table_block = tables[lon_block]
        grid_values = (
            jnp.einsum("flac,cb->flab", spec_block, table_block, preferred_element_type=jnp.float32)
            * inv_orders
        )
        lamb_vector = cross_product(grid_values[:3], grid_values[3:])
        accumulated = accumulated + jnp.einsum(
            "flab,cb->flac",
            lamb_vector,
            table_block.astype(jnp.float32),
            precision=lax.Precision.HIGH,
            preferred_element_type=jnp.float32,
        )
    lamb_spec = (accumulated * inv_lon).astype(jnp.bfloat16)
    selector = jnp.transpose(mask_bool.astype(jnp.float32), (1, 0, 2, 3))[:, None, None, None]
    lamb_block = lax.all_to_all(lamb_spec, "ma", split_axis=3, concat_axis=2, tiled=True)
    item_count = lamb_block.shape[0]
    shaped = lamb_block.astype(jnp.float32).reshape(
        item_count, levels_dev, nlat_all, 2, 2, pair_count
    )
    shaped = jnp.transpose(shaped, (0, 1, 3, 4, 5, 2))
    north_side = shaped[..., :half_lat]
    south_side = shaped[..., half_lat:]
    weighted = jnp.stack(
        [lat_weight * (north_side + south_side), lat_weight * (north_side - south_side)]
    )
    weighted = weighted.astype(jnp.bfloat16)
    projected = jnp.einsum(
        "qfliosj,srj->qfliosr", weighted, legendre, preferred_element_type=jnp.float32
    )
    picked = jnp.sum(projected * selector, axis=(0, 4))
    tendency = jnp.transpose(picked, (0, 2, 1, 3, 4))
    source = velocity.astype(jnp.float32) + STEP_SIZE * tendency
    row_start = lax.axis_index("row") * levels_dev
    level_total = levels_dev * lax.axis_size("row")
    extended = with_halo(source.astype(jnp.bfloat16), (("row", 2),), 2).astype(source.dtype)
    padded_coupling = jnp.pad(diffusivity, (2, 2))
    wide_coupling = lax.dynamic_slice_in_dim(padded_coupling, row_start, levels_dev + 4)[
        None, None, :, None, None
    ]
    inner_coupling = wide_coupling[:, :, 1:-1]
    first_wide = (
        extended[:, :, 1:-1] + inner_coupling * (extended[:, :, :-2] + extended[:, :, 2:])
    ) / (1.0 + 2.0 * inner_coupling)
    global_level = row_start - 1 + jnp.arange(levels_dev + 2, dtype=jnp.int32)
    inside = ((global_level >= 0) & (global_level < level_total)).astype(jnp.float32)
    first_wide = first_wide * inside[None, None, :, None, None]
    own_coupling = wide_coupling[:, :, 2:-2]
    return (source + own_coupling * (first_wide[:, :, :-2] + first_wide[:, :, 2:])) / (
        1.0 + 2.0 * own_coupling
    )

def lon_count(orders_all):
    need = 3 * (orders_all - 1) + 1
    return min(NLON, -(-need // 128) * 128)


def pack_lanes(pair_count, pack_rows):
    return -(-(pair_count * pack_rows + pair_count) // 128) * 128


def remote(src, dst, send_sem, recv_sem, device_id):
    return pltpu.make_async_remote_copy(
        src_ref=src,
        dst_ref=dst,
        send_sem=send_sem,
        recv_sem=recv_sem,
        device_id=device_id,
        device_id_type=pl.DeviceIdType.MESH,
    )


def fused_kernel(
    n_ma, n_row, pairs, rows, levels,
    coef_ref, leg_ref, weight_ref, dif_ref, tab_ref, tab_t_ref,
    out_ref,
    coef_all, leg_all, onehot, spec, wgt, part, part_in, ext,
    coef_send, coef_recv, leg_send, leg_recv, part_send, part_recv, halo_send, halo_recv,
):
    me = lax.axis_index("ma")
    row = lax.axis_index("row")
    lanes = coef_ref.shape[1]
    groups = coef_ref.shape[0]
    fields2 = groups // 2
    orders = rows - 1
    slots = 2 * pairs
    lat = leg_ref.shape[1]
    used = pairs * rows
    f32 = jnp.float32
    bf16 = jnp.bfloat16
    left = lax.rem(row + n_row - 1, n_row)
    right = lax.rem(row + 1, n_row)

    barrier = pltpu.get_barrier_semaphore()
    for d in range(1, n_ma):
        pl.semaphore_signal(
            barrier, inc=1, device_id=(lax.rem(me + d, n_ma), row), device_id_type=pl.DeviceIdType.MESH
        )
    for side in (left, right):
        pl.semaphore_signal(barrier, inc=1, device_id=(me, side), device_id_type=pl.DeviceIdType.MESH)
    pl.semaphore_wait(barrier, n_ma + 1)

    def coef_copy(d):
        peer = lax.rem(me + d, n_ma)
        return remote(coef_ref, coef_all.at[d], coef_send.at[d], coef_recv.at[d], (peer, row))

    def leg_copy(d):
        peer = lax.rem(me + d, n_ma)
        return remote(leg_ref.at[peer], leg_all.at[d], leg_send.at[d], leg_recv.at[d], (peer, row))

    for d in range(1, n_ma):
        coef_copy(d).start()
        leg_copy(d).start()

    coef_all[0] = coef_ref[...]
    leg_all[0] = leg_ref[me]

    lane = lax.broadcasted_iota(jnp.int32, (slots, lanes), 1)
    sub = lax.broadcasted_iota(jnp.int32, (slots, lanes), 0)
    lane_pair = jnp.zeros((slots, lanes), jnp.int32)
    for p in range(1, pairs):
        lane_pair = lane_pair + (lane >= p * rows).astype(jnp.int32)
    lane_row = lane - rows * lane_pair
    own = (lane_pair == sub // 2) & (lane < used)
    is_high = (sub % 2) == 1
    m_lane = lax.broadcasted_iota(jnp.int32, (slots, orders), 1)
    m_sub = lax.broadcasted_iota(jnp.int32, (slots, orders), 0)

    def lows(d):
        head = coef_all[d, 0:16, :].astype(f32)
        return [head[0:1, used + p : used + p + 1].astype(jnp.int32) for p in range(pairs)]

    def masks(d):
        values = lows(d)
        low = jnp.zeros((slots, lanes), jnp.int32)
        for p in range(pairs):
            low = jnp.where(lane_pair == p, values[p], low)
        lower = lane_row < orders - low
        picked = own & jnp.logical_xor(is_high, lower)
        parity = jnp.where(is_high, lane_row + low, lane_row) & 1
        even = (picked & (parity == 0)).astype(f32)
        odd = (picked & (parity == 1)).astype(f32)
        return even, odd

    def synth(d, carry):
        values = lows(d)
        order = jnp.zeros((slots, orders), jnp.int32)
        for p in range(pairs):
            order = jnp.where(m_sub == 2 * p, values[p], order)
            order = jnp.where(m_sub == 2 * p + 1, orders - 1 - values[p], order)
        base = pl.multiple_of(d * slots, slots)
        onehot[pl.ds(base, slots), :] = (m_lane == order).astype(f32)
        even, odd = masks(d)
        coef = coef_all[d].astype(f32)
        leg = leg_all[d]
        for h in range(2):
            mask = even + odd if h == 0 else even - odd
            lhs = (coef[:, None, :] * mask[None]).reshape(groups * slots, lanes).astype(bf16)
            made = lax.dot_general(lhs, leg, (((1,), (1,)), ((), ())), preferred_element_type=f32)
            spec[h, :, :, pl.ds(base, slots), :] = made.reshape(fields2, 2, slots, lat)
        return carry

    synth(0, 0)
    def arrive(d, carry):
        coef_copy(d).wait_recv()
        leg_copy(d).wait_recv()
        return synth(d, carry)
    lax.fori_loop(1, n_ma, arrive, 0)

    hot = onehot[...].astype(bf16)
    full = n_ma * slots
    to_grid = jnp.concatenate(
        [
            lax.dot_general(tab_t_ref[c], hot, (((1,), (1,)), ((), ())), preferred_element_type=f32)
            for c in range(2)
        ],
        axis=1,
    ).astype(bf16)
    to_spec = jnp.concatenate(
        [jnp.dot(hot, tab_ref[c], preferred_element_type=f32) for c in range(2)], axis=0
    ).astype(bf16)
    weight = weight_ref[...]

    def middle(k, carry):
        halves = []
        for h in range(2):
            grids = []
            for g in range(2):
                for f in range(3):
                    block = spec[h, g * 3 * levels + k * 3 + f].reshape(2 * full, lat).astype(bf16)
                    grids.append(jnp.dot(to_grid, block, preferred_element_type=f32))
            u, w = grids[:3], grids[3:]
            lamb = [
                u[1] * w[2] - u[2] * w[1],
                u[2] * w[0] - u[0] * w[2],
                u[0] * w[1] - u[1] * w[0],
            ]
            halves.append(
                [jnp.dot(to_spec, x.astype(bf16), preferred_element_type=f32) for x in lamb]
            )
        for f in range(3):
            north, south = halves[0][f], halves[1][f]
            wgt[0, k * 3 + f] = (weight * (north + south)).reshape(2, full, lat)
            wgt[1, k * 3 + f] = (weight * (north - south)).reshape(2, full, lat)
        return carry

    lax.fori_loop(0, levels, middle, 0)

    def part_copy(d):
        peer = lax.rem(me + n_ma - d, n_ma)
        return remote(part.at[d], part_in.at[d], part_send.at[d], part_recv.at[d], (peer, row))

    def analyse(d):
        base = pl.multiple_of(d * slots, slots)
        total = None
        for q, mask in enumerate(masks(d)):
            lhs = wgt[q, :, :, pl.ds(base, slots), :].reshape(fields2 * slots, lat).astype(bf16)
            made = jnp.dot(lhs, leg_all[d], preferred_element_type=f32)
            made = made.reshape(fields2, slots, lanes) * mask[None]
            total = made if total is None else total + made
        return jnp.sum(total, axis=1)

    def project(i, carry):
        d = n_ma - i
        part[d] = analyse(d).astype(bf16)
        part_copy(d).start()
        return carry

    lax.fori_loop(1, n_ma, project, 0)
    source = analyse(0) + coef_ref[0:fields2, :].astype(f32)

    def gather(i, total):
        d = n_ma - i
        part_copy(d).wait_recv()
        return total + part_in[d].astype(f32)

    source = lax.fori_loop(1, n_ma, gather, source)
    source = source.reshape(levels, fields2 // levels, lanes)
    ext[2 : levels + 2] = source
    to_left = remote(ext.at[2:4], ext.at[levels + 2 : levels + 4], halo_send.at[0], halo_recv.at[0], (me, left))
    to_right = remote(ext.at[levels : levels + 2], ext.at[0:2], halo_send.at[1], halo_recv.at[1], (me, right))
    to_left.start()
    to_right.start()

    def drain(d, carry):
        coef_copy(d).wait_send()
        leg_copy(d).wait_send()
        part_copy(d).wait_send()
        return carry

    lax.fori_loop(1, n_ma, drain, 0)
    to_left.wait()
    to_right.wait()

    shape = (fields2 // levels, lanes)
    has_left = (row > 0).astype(f32)
    has_right = (row < n_row - 1).astype(f32)
    wide = [ext[i] for i in range(levels + 4)]
    for i in range(2):
        wide[i] = wide[i] * has_left
        wide[levels + 2 + i] = wide[levels + 2 + i] * has_right
    coupling = [jnp.full(shape, dif_ref[row * levels + i]) for i in range(levels + 4)]
    inverse = [1.0 / (1.0 + 2.0 * c) for c in coupling]
    first = [
        (wide[i] + coupling[i] * (wide[i - 1] + wide[i + 1])) * inverse[i] for i in range(1, levels + 3)
    ]
    first[0] = first[0] * has_left
    first[-1] = first[-1] * has_right
    for k in range(levels):
        done = (wide[k + 2] + coupling[k + 2] * (first[k] + first[k + 2])) * inverse[k + 2]
        out_ref[k] = done[:, :used]


def fused(velocity, vorticity, legendre, pair_order, lat_weight, diffusivity):
    n_ma = lax.axis_size("ma")
    n_row = lax.axis_size("row")
    pairs, rows, half_lat = legendre.shape
    levels = velocity.shape[2]
    orders = rows - 1
    used = pairs * rows
    lanes = pack_lanes(pairs, rows)
    lat = half_lat // n_ma
    slots = 2 * pairs
    full = n_ma * slots
    points = lon_count(orders)
    bf16 = jnp.bfloat16
    f32 = jnp.float32

    def packed(x):
        return jnp.transpose(x, (2, 0, 1, 3, 4)).reshape(levels * 6, used)

    groups = 12 * levels
    coef = jnp.concatenate(
        [
            jnp.concatenate([packed(velocity), packed(vorticity)], axis=0),
            jnp.broadcast_to(pair_order.astype(bf16)[None], (groups, pairs)),
            jnp.zeros((groups, lanes - used - pairs), bf16),
        ],
        axis=1,
    )
    leg = jnp.transpose(legendre.reshape(used, half_lat))
    leg = jnp.pad(leg, ((0, 0), (0, lanes - used))).reshape(n_ma, lat, lanes)
    scale = (NLON / points) / math.sqrt(NLON) / orders
    weight = lax.dynamic_slice_in_dim(lat_weight, lax.axis_index("ma") * lat, lat) * scale
    angle = np.outer(np.arange(orders), np.arange(points)) % points * (2.0 * math.pi / points)
    table = np.stack([np.cos(angle), -np.sin(angle)])
    tab = jnp.asarray(table, bf16)
    tab_t = jnp.asarray(np.transpose(table, (0, 2, 1)), bf16)
    vmem = pl.BlockSpec(memory_space=pltpu.VMEM)
    out = pl.pallas_call(
        functools.partial(fused_kernel, n_ma, n_row, pairs, rows, levels),
        out_shape=jax.ShapeDtypeStruct((levels, 6, used), f32),
        in_specs=[vmem, vmem, vmem, pl.BlockSpec(memory_space=pltpu.SMEM), vmem, vmem],
        out_specs=vmem,
        scratch_shapes=[
            pltpu.VMEM((n_ma, groups, lanes), bf16),
            pltpu.VMEM((n_ma, lat, lanes), bf16),
            pltpu.VMEM((full, orders), f32),
            pltpu.VMEM((2, groups // 2, 2, full, lat), f32),
            pltpu.VMEM((2, 3 * levels, 2, full, lat), f32),
            pltpu.VMEM((n_ma, groups // 2, lanes), bf16),
            pltpu.VMEM((n_ma, groups // 2, lanes), bf16),
            pltpu.VMEM((levels + 4, 6, lanes), f32),
        ]
        + [pltpu.SemaphoreType.DMA((n_ma,))] * 6
        + [pltpu.SemaphoreType.DMA((2,))] * 2,
        compiler_params=pltpu.CompilerParams(
            collective_id=0, has_side_effects=True, vmem_limit_bytes=48 * 1024 * 1024
        ),
    )(coef, leg, weight[None], jnp.pad(diffusivity, (2, 2)), tab, tab_t)
    return jnp.transpose(out.reshape(levels, 3, 2, pairs, rows), (1, 2, 0, 3, 4))


def fits(velocity, legendre):
    n_ma = lax.axis_size("ma")
    n_row = lax.axis_size("row")
    pairs, rows, half_lat = legendre.shape
    levels = velocity.shape[2]
    small = rows <= 129 and pairs * n_ma <= 128 and half_lat // n_ma <= 128
    whole = half_lat % n_ma == 0 and half_lat // n_ma % 16 == 0 and pairs % 4 == 0 and levels % 4 == 0
    return small and whole and n_row > 2 and n_ma > 1


def step(velocity, vorticity, legendre, pair_order, lat_weight, diffusivity):
    chosen = fused if fits(velocity, legendre) else local
    return chosen(velocity, vorticity, legendre, pair_order, lat_weight, diffusivity)


def solution(mesh):
    in_specs = (
        P(None, None, "row", "ma", None),
        P(None, None, "row", "ma", None),
        P("ma", None, None),
        P("ma"),
        P(),
        P(),
    )
    out_specs = P(None, None, "row", "ma", None)
    return jax.shard_map(step, mesh=mesh, in_specs=in_specs, out_specs=out_specs, check_vma=False)
```

```python
import functools
import math

import jax
import jax.numpy as jnp
import numpy as np
from jax import lax
from jax.experimental import pallas as pl
from jax.experimental.pallas import tpu as pltpu
from jax.sharding import PartitionSpec as P

NLON = 2048


STEP_SIZE = 1.0


def with_halo(cells, sides, width):
    for axis, dim in sides:
        count = lax.axis_size(axis)
        ends = count - 1
        head = lax.slice_in_dim(cells, 0, width, axis=dim)
        tail = lax.slice_in_dim(cells, cells.shape[dim] - width, cells.shape[dim], axis=dim)
        cells = jnp.concatenate(
            [
                lax.ppermute(tail, axis, [(i, (i + 1) % count) for i in range(ends)]),
                cells,
                lax.ppermute(head, axis, [((i + 1) % count, i) for i in range(ends)]),
            ],
            axis=dim,
        )
    return cells


def row_masks(low_order, pack_rows):
    orders_all = pack_rows - 1
    row_index = jnp.arange(pack_rows, dtype=jnp.int32)[None, :]
    low_column = low_order[:, None]
    is_lower = row_index < orders_all - low_column
    not_lower = jnp.logical_not(is_lower)
    even_low = row_index % 2 == 0
    even_high = (row_index + low_column) % 2 == 0
    low_pair = jnp.stack([is_lower & even_low, is_lower & jnp.logical_not(even_low)])
    high_pair = jnp.stack([not_lower & even_high, not_lower & jnp.logical_not(even_high)])
    return jnp.stack([low_pair, high_pair])


def cross_product(velocity_grid, vorticity_grid):
    return jnp.stack(
        [
            velocity_grid[1] * vorticity_grid[2] - velocity_grid[2] * vorticity_grid[1],
            velocity_grid[2] * vorticity_grid[0] - velocity_grid[0] * vorticity_grid[2],
            velocity_grid[0] * vorticity_grid[1] - velocity_grid[1] * vorticity_grid[0],
        ]
    )


def lon_table(column_order, is_imag, lon_start, lon_count):
    lon_index = lon_start + jnp.arange(lon_count, dtype=jnp.int32)
    angle_index = column_order[:, None] * lon_index[None, :] % NLON
    angle_value = angle_index.astype(jnp.float32) * (2.0 * math.pi / NLON)
    return jnp.where(is_imag[:, None], -jnp.sin(angle_value), jnp.cos(angle_value))


def local(velocity, vorticity, legendre, pair_order, lat_weight, diffusivity):
    pair_count = pair_order.shape[0]
    pack_rows = legendre.shape[1]
    half_lat = legendre.shape[2]
    nlat_all = 2 * half_lat
    levels_dev = velocity.shape[2]
    orders_all = pack_rows - 1
    inv_orders = 1.0 / math.sqrt(orders_all)
    inv_lon = 1.0 / math.sqrt(NLON)
    lon_width = NLON // 4
    mask_bool = row_masks(pair_order, pack_rows)
    fields = jnp.concatenate([velocity, vorticity], axis=0)
    masked = fields[None, None] * mask_bool.astype(jnp.bfloat16)[:, :, None, None, None]
    halves = jnp.einsum(
        "oqfilsr,srj->qfliosj", masked, legendre, preferred_element_type=jnp.float32
    )
    north_part = halves[0] + halves[1]
    south_part = halves[0] - halves[1]
    both_parts = jnp.concatenate([north_part, south_part], axis=-1)
    spectral = jnp.transpose(both_parts, (0, 1, 5, 2, 3, 4))
    spectral = spectral.reshape(6, levels_dev, nlat_all, 4 * pair_count).astype(jnp.bfloat16)
    gathered_ids = lax.all_gather(pair_order, "ma", axis=0, tiled=True)
    pair_slots = gathered_ids.reshape(-1, 1, 1, pair_count)
    both_orders = jnp.concatenate([pair_slots, orders_all - 1 - pair_slots], axis=2)
    full_shape = (both_orders.shape[0], 2, 2, pair_count)
    column_order = jnp.broadcast_to(both_orders, full_shape).reshape(-1)
    part_index = jnp.arange(2, dtype=jnp.int32)[None, :, None, None]
    is_imag = jnp.broadcast_to(part_index, full_shape).reshape(-1) == 1
    tables = [
        lon_table(column_order, is_imag, lon_block * lon_width, lon_width).astype(jnp.bfloat16)
        for lon_block in range(4)
    ]
    spec_block = lax.all_to_all(spectral, "ma", split_axis=2, concat_axis=3, tiled=True)
    accumulated = jnp.zeros((3,) + spec_block.shape[1:], jnp.float32)
    for lon_block in range(4):
        table_block = tables[lon_block]
        grid_values = (
            jnp.einsum("flac,cb->flab", spec_block, table_block, preferred_element_type=jnp.float32)
            * inv_orders
        )
        lamb_vector = cross_product(grid_values[:3], grid_values[3:])
        accumulated = accumulated + jnp.einsum(
            "flab,cb->flac",
            lamb_vector,
            table_block.astype(jnp.float32),
            precision=lax.Precision.HIGH,
            preferred_element_type=jnp.float32,
        )
    lamb_spec = (accumulated * inv_lon).astype(jnp.bfloat16)
    selector = jnp.transpose(mask_bool.astype(jnp.float32), (1, 0, 2, 3))[:, None, None, None]
    lamb_block = lax.all_to_all(lamb_spec, "ma", split_axis=3, concat_axis=2, tiled=True)
    item_count = lamb_block.shape[0]
    shaped = lamb_block.astype(jnp.float32).reshape(
        item_count, levels_dev, nlat_all, 2, 2, pair_count
    )
    shaped = jnp.transpose(shaped, (0, 1, 3, 4, 5, 2))
    north_side = shaped[..., :half_lat]
    south_side = shaped[..., half_lat:]
    weighted = jnp.stack(
        [lat_weight * (north_side + south_side), lat_weight * (north_side - south_side)]
    )
    weighted = weighted.astype(jnp.bfloat16)
    projected = jnp.einsum(
        "qfliosj,srj->qfliosr", weighted, legendre, preferred_element_type=jnp.float32
    )
    picked = jnp.sum(projected * selector, axis=(0, 4))
    tendency = jnp.transpose(picked, (0, 2, 1, 3, 4))
    source = velocity.astype(jnp.float32) + STEP_SIZE * tendency
    row_start = lax.axis_index("row") * levels_dev
    level_total = levels_dev * lax.axis_size("row")
    extended = with_halo(source.astype(jnp.bfloat16), (("row", 2),), 2).astype(source.dtype)
    padded_coupling = jnp.pad(diffusivity, (2, 2))
    wide_coupling = lax.dynamic_slice_in_dim(padded_coupling, row_start, levels_dev + 4)[
        None, None, :, None, None
    ]
    inner_coupling = wide_coupling[:, :, 1:-1]
    first_wide = (
        extended[:, :, 1:-1] + inner_coupling * (extended[:, :, :-2] + extended[:, :, 2:])
    ) / (1.0 + 2.0 * inner_coupling)
    global_level = row_start - 1 + jnp.arange(levels_dev + 2, dtype=jnp.int32)
    inside = ((global_level >= 0) & (global_level < level_total)).astype(jnp.float32)
    first_wide = first_wide * inside[None, None, :, None, None]
    own_coupling = wide_coupling[:, :, 2:-2]
    return (source + own_coupling * (first_wide[:, :, :-2] + first_wide[:, :, 2:])) / (
        1.0 + 2.0 * own_coupling
    )

def lon_count(orders_all):
    need = 3 * (orders_all - 1) + 1
    return min(NLON, -(-need // 128) * 128)


def remote(src, dst, send_sem, recv_sem, device_id):
    return pltpu.make_async_remote_copy(
        src_ref=src,
        dst_ref=dst,
        send_sem=send_sem,
        recv_sem=recv_sem,
        device_id=device_id,
        device_id_type=pl.DeviceIdType.MESH,
    )


def fused_kernel(
    n_ma, n_row, pairs, rows, levels,
    coef_ref, leg_ref, rest_ref, weight_ref, dif_ref, tab_ref, tab_t_ref,
    out_ref,
    coef_all, leg_all, rest_all, rest_t, onehot, spec, wgt, part, part_in, ext,
    coef_send, coef_recv, leg_send, leg_recv, swap_send, swap_recv, rest_send, rest_recv, part_send, part_recv, halo_send, halo_recv,
):
    me = lax.axis_index("ma")
    row = lax.axis_index("row")
    chunks, groups, wide_lanes = coef_ref.shape
    lanes = (chunks + 1) * wide_lanes
    fields2 = groups // 2
    orders = rows - 1
    slots = 2 * pairs
    lat = leg_ref.shape[2]
    main = pairs * orders
    f32 = jnp.float32
    bf16 = jnp.bfloat16
    n_z = n_ma // 2
    z, y = me // 2, lax.rem(me, 2)
    mate = me + 1 - 2 * y
    half = lax.rem(row, 2)
    mate_row = row + 1 - 2 * half

    def target(s):
        return lax.rem(z + s // 2, n_z) * 2 + lax.rem(y + lax.rem(s, 2), 2)

    def origin(s):
        return lax.rem(z + n_z - s // 2, n_z) * 2 + lax.rem(y + lax.rem(s, 2), 2)

    left = lax.rem(row + n_row - 1, n_row)
    right = lax.rem(row + 1, n_row)

    barrier = pltpu.get_barrier_semaphore()
    for d in range(1, n_ma):
        pl.semaphore_signal(
            barrier, inc=1, device_id=(lax.rem(me + d, n_ma), row), device_id_type=pl.DeviceIdType.MESH
        )
    for side in (left, right):
        pl.semaphore_signal(barrier, inc=1, device_id=(me, side), device_id_type=pl.DeviceIdType.MESH)
    pl.semaphore_wait(barrier, n_ma + 1)

    def coef_copy(s):
        if s % 2 == 0:
            return remote(coef_ref, coef_all.at[s], coef_send.at[s], coef_recv.at[s], (target(s), row))
        src = coef_ref if s == 1 else coef_all.at[s - 1]
        return remote(src, coef_all.at[s], coef_send.at[s], coef_recv.at[s], (mate, row))

    def leg_copy(s):
        peer = target(s)
        return remote(
            leg_ref.at[peer, half], leg_all.at[s, half], leg_send.at[s], leg_recv.at[s], (peer, row)
        )

    def swap_copy(s):
        return remote(
            leg_all.at[s, half], leg_all.at[s, half], swap_send.at[s], swap_recv.at[s], (me, mate_row)
        )

    def rest_copy(s):
        peer = target(s)
        return remote(rest_ref.at[peer], rest_all.at[s], rest_send.at[s], rest_recv.at[s], (peer, row))

    for s in range(1, n_ma):
        rest_copy(s).start()
    for s in range(n_ma - 2, 0, -2):
        coef_copy(s).start()
        leg_copy(s).start()
        leg_copy(s + 1).start()
    coef_copy(1).start()
    leg_copy(1).start()

    coef_all[0] = coef_ref[...]
    leg_all[0] = leg_ref[me]
    rest_all[0] = rest_ref[me]

    lane = lax.broadcasted_iota(jnp.int32, (slots, lanes), 1)
    sub = lax.broadcasted_iota(jnp.int32, (slots, lanes), 0)
    is_high = (sub % 2) == 1
    m_lane = lax.broadcasted_iota(jnp.int32, (slots, orders), 1)
    m_sub = lax.broadcasted_iota(jnp.int32, (slots, orders), 0)

    def lows(d):
        tile = rest_all[d].astype(jnp.float32)
        return [tile[pairs + p : pairs + p + 1, 0:1].astype(jnp.int32) for p in range(pairs)]

    def masks(d):
        values = lows(d)
        extra = lane - main - 8 * d
        in_main = lane < main
        lane_pair = jnp.where(in_main, lane // orders, extra)
        lane_row = jnp.where(in_main, lane % orders, orders)
        own = lane_pair == sub // 2
        low = jnp.zeros((slots, lanes), jnp.int32)
        for p in range(pairs):
            low = jnp.where(lane_pair == p, values[p], low)
        lower = lane_row < orders - low
        picked = own & jnp.logical_xor(is_high, lower)
        parity = jnp.where(is_high, lane_row + low, lane_row) & 1
        even = (picked & (parity == 0)).astype(f32)
        odd = (picked & (parity == 1)).astype(f32)
        return even, odd

    def leg_of(d):
        tail = rest_t[wide_lanes // 2 : wide_lanes // 2 + lat, :].astype(bf16)
        return jnp.concatenate([leg_all[d, c] for c in range(chunks)] + [tail], axis=1)

    def synth(d, carry):
        values = lows(d)
        order = jnp.zeros((slots, orders), jnp.int32)
        for p in range(pairs):
            order = jnp.where(m_sub == 2 * p, values[p], order)
            order = jnp.where(m_sub == 2 * p + 1, orders - 1 - values[p], order)
        base = pl.multiple_of(d * slots, slots)
        onehot[pl.ds(base, slots), :] = (m_lane == order).astype(f32)
        even, odd = masks(d)
        coef = jnp.concatenate(
            [coef_all[d, c].astype(f32) for c in range(chunks)] + [rest_t[0:groups, :]], axis=1
        )
        leg = leg_of(d)
        for h in range(2):
            mask = even + odd if h == 0 else even - odd
            lhs = (coef[:, None, :] * mask[None]).reshape(groups * slots, lanes).astype(bf16)
            made = lax.dot_general(lhs, leg, (((1,), (1,)), ((), ())), preferred_element_type=f32)
            spec[h, :, :, pl.ds(base, slots), :] = made.reshape(fields2, 2, slots, lat)
        return carry

    for s in range(1, n_ma):
        rest_copy(s).wait_recv()
    rest = rest_all[...].astype(f32).reshape(n_ma * 8, wide_lanes)
    rest = jnp.concatenate([rest, jnp.zeros((wide_lanes - n_ma * 8, wide_lanes), f32)], axis=0)
    rest_t[...] = jnp.transpose(rest)
    leg_copy(1).wait_recv()
    swap_copy(1).start()
    for s in range(2, n_ma, 2):
        coef_copy(s).wait_recv()
        coef_copy(s + 1).start()
        for t in (s, s + 1):
            leg_copy(t).wait_recv()
            swap_copy(t).start()
    synth(0, 0)
    for s in range(1, n_ma):
        if s % 2 == 1:
            coef_copy(s).wait_recv()
        remote(
            leg_all.at[s, half], leg_all.at[s, 1 - half], swap_send.at[s], swap_recv.at[s], (me, mate_row)
        ).wait_recv()
        synth(s, 0)

    hot = onehot[...].astype(bf16)
    full = n_ma * slots
    to_grid = jnp.concatenate(
        [
            lax.dot_general(tab_t_ref[c], hot, (((1,), (1,)), ((), ())), preferred_element_type=f32)
            for c in range(2)
        ],
        axis=1,
    ).astype(bf16)
    to_spec = jnp.concatenate(
        [jnp.dot(hot, tab_ref[c], preferred_element_type=f32) for c in range(2)], axis=0
    ).astype(bf16)
    weight = weight_ref[...]

    def middle(k, carry):
        halves = []
        for h in range(2):
            grids = []
            for g in range(2):
                for f in range(3):
                    block = spec[h, g * 3 * levels + k * 3 + f].reshape(2 * full, lat).astype(bf16)
                    grids.append(jnp.dot(to_grid, block, preferred_element_type=f32))
            u, w = grids[:3], grids[3:]
            lamb = [
                u[1] * w[2] - u[2] * w[1],
                u[2] * w[0] - u[0] * w[2],
                u[0] * w[1] - u[1] * w[0],
            ]
            halves.append(
                [jnp.dot(to_spec, x.astype(bf16), preferred_element_type=f32) for x in lamb]
            )
        for f in range(3):
            north, south = halves[0][f], halves[1][f]
            wgt[0, k * 3 + f] = (weight * (north + south)).reshape(2, full, lat)
            wgt[1, k * 3 + f] = (weight * (north - south)).reshape(2, full, lat)
        return carry

    lax.fori_loop(0, levels, middle, 0)

    def part_copy(d):
        return remote(part.at[d], part_in.at[d], part_send.at[d], part_recv.at[d], (origin(d), row))

    def analyse(d):
        base = pl.multiple_of(d * slots, slots)
        total = None
        for q, mask in enumerate(masks(d)):
            lhs = wgt[q, :, :, pl.ds(base, slots), :].reshape(fields2 * slots, lat).astype(bf16)
            made = jnp.dot(lhs, leg_of(d), preferred_element_type=f32)
            made = made.reshape(fields2, slots, lanes) * mask[None]
            total = made if total is None else total + made
        return jnp.sum(total, axis=1)

    def project(i, carry):
        d = n_ma - i
        part[d] = analyse(d).astype(bf16)
        part_copy(d).start()
        return carry

    lax.fori_loop(1, n_ma, project, 0)
    source = analyse(0)

    def gather(i, total):
        d = n_ma - i
        part_copy(d).wait_recv()
        return total + part_in[d].astype(f32)

    source = lax.fori_loop(1, n_ma, gather, source)
    tail = source[:, main:]
    for shift in (8, 16, 32):
        tail = tail + pltpu.roll(tail, wide_lanes - shift, 1)
    own_tail = rest_t[0:fields2, :]
    heads = [source[:, c * wide_lanes : (c + 1) * wide_lanes] + coef_ref[c, 0:fields2].astype(f32) for c in range(chunks)]
    source = jnp.concatenate(heads + [tail + own_tail], axis=1)
    source = source.reshape(levels, fields2 // levels, lanes)
    ext[2 : levels + 2] = source
    to_left = remote(ext.at[2:4], ext.at[levels + 2 : levels + 4], halo_send.at[0], halo_recv.at[0], (me, left))
    to_right = remote(ext.at[levels : levels + 2], ext.at[0:2], halo_send.at[1], halo_recv.at[1], (me, right))
    to_left.start()
    to_right.start()

    for s in range(1, n_ma):
        coef_copy(s).wait_send()
        leg_copy(s).wait_send()
        swap_copy(s).wait_send()
        rest_copy(s).wait_send()
        part_copy(s).wait_send()
    to_left.wait()
    to_right.wait()

    shape = (fields2 // levels, lanes)
    has_left = (row > 0).astype(f32)
    has_right = (row < n_row - 1).astype(f32)
    wide = [ext[i] for i in range(levels + 4)]
    for i in range(2):
        wide[i] = wide[i] * has_left
        wide[levels + 2 + i] = wide[levels + 2 + i] * has_right
    coupling = [jnp.full(shape, dif_ref[row * levels + i]) for i in range(levels + 4)]
    inverse = [1.0 / (1.0 + 2.0 * c) for c in coupling]
    first = [
        (wide[i] + coupling[i] * (wide[i - 1] + wide[i + 1])) * inverse[i] for i in range(1, levels + 3)
    ]
    first[0] = first[0] * has_left
    first[-1] = first[-1] * has_right
    for k in range(levels):
        done = (wide[k + 2] + coupling[k + 2] * (first[k] + first[k + 2])) * inverse[k + 2]
        out_ref[k] = done[:, : main + pairs]


def fused(velocity, vorticity, legendre, pair_order, lat_weight, diffusivity):
    n_ma = lax.axis_size("ma")
    n_row = lax.axis_size("row")
    pairs, rows, half_lat = legendre.shape
    levels = velocity.shape[2]
    orders = rows - 1
    main = pairs * orders
    used = main + pairs
    chunks = main // 128
    lanes = main + 128
    lat = half_lat // n_ma
    slots = 2 * pairs
    full = n_ma * slots
    points = lon_count(orders)
    bf16 = jnp.bfloat16
    f32 = jnp.float32
    groups = 12 * levels
    heads, tails = [], []
    for x in (velocity, vorticity):
        x = jnp.transpose(x, (2, 0, 1, 3, 4))
        heads.append(x[..., :orders].reshape(6 * levels, chunks, 128))
        tails.append(x[..., orders].reshape(6 * levels, pairs))
    coef = jnp.transpose(jnp.concatenate(heads, axis=0), (1, 0, 2))
    leg = legendre[:, :orders].reshape(chunks, 128, n_ma, lat)
    leg = jnp.transpose(leg, (2, 0, 3, 1))
    coef_tail = jnp.transpose(jnp.concatenate(tails, axis=0))
    coef_tail = jnp.pad(coef_tail, ((0, 0), (0, 64 - groups)))
    leg_tail = jnp.transpose(legendre[:, orders].reshape(pairs, n_ma, lat), (1, 0, 2))
    leg_tail = jnp.pad(leg_tail, ((0, 0), (0, 0), (0, 64 - lat)))
    tail = jnp.concatenate([jnp.broadcast_to(coef_tail, (n_ma, pairs, 64)), leg_tail], axis=2)
    order_rows = jnp.broadcast_to(pair_order.astype(bf16)[None, :, None], (n_ma, pairs, 128))
    rest = jnp.concatenate([tail, order_rows], axis=1)
    scale = (NLON / points) / math.sqrt(NLON) / orders
    weight = lax.dynamic_slice_in_dim(lat_weight, lax.axis_index("ma") * lat, lat) * scale
    angle = np.outer(np.arange(orders), np.arange(points)) % points * (2.0 * math.pi / points)
    table = np.stack([np.cos(angle), -np.sin(angle)])
    tab = jnp.asarray(table, bf16)
    tab_t = jnp.asarray(np.transpose(table, (0, 2, 1)), bf16)
    vmem = pl.BlockSpec(memory_space=pltpu.VMEM)
    out = pl.pallas_call(
        functools.partial(fused_kernel, n_ma, n_row, pairs, rows, levels),
        out_shape=jax.ShapeDtypeStruct((levels, 6, used), f32),
        in_specs=[vmem, vmem, vmem, vmem, pl.BlockSpec(memory_space=pltpu.SMEM), vmem, vmem],
        out_specs=vmem,
        scratch_shapes=[
            pltpu.VMEM((n_ma, chunks, groups, 128), bf16),
            pltpu.VMEM((n_ma, chunks, lat, 128), bf16),
            pltpu.VMEM((n_ma, 8, 128), bf16),
            pltpu.VMEM((128, 128), f32),
            pltpu.VMEM((full, orders), f32),
            pltpu.VMEM((2, groups // 2, 2, full, lat), f32),
            pltpu.VMEM((2, 3 * levels, 2, full, lat), f32),
            pltpu.VMEM((n_ma, groups // 2, lanes), bf16),
            pltpu.VMEM((n_ma, groups // 2, lanes), bf16),
            pltpu.VMEM((levels + 4, 6, lanes), f32),
        ]
        + [pltpu.SemaphoreType.DMA((n_ma,))] * 10
        + [pltpu.SemaphoreType.DMA((2,))] * 2,
        compiler_params=pltpu.CompilerParams(
            collective_id=0, has_side_effects=True, vmem_limit_bytes=48 * 1024 * 1024
        ),
    )(coef, leg, rest, weight[None], jnp.pad(diffusivity, (2, 2)), tab, tab_t)
    out = jnp.concatenate(
        [out[..., :main].reshape(levels, 6, pairs, orders), out[..., main:, None]], axis=3
    )
    return jnp.transpose(out.reshape(levels, 3, 2, pairs, rows), (1, 2, 0, 3, 4))


def fits(velocity, legendre):
    n_ma = lax.axis_size("ma")
    n_row = lax.axis_size("row")
    pairs, rows, half_lat = legendre.shape
    levels = velocity.shape[2]
    lat = half_lat // n_ma
    tiles = pairs == 4 and pairs * (rows - 1) == 256 and n_ma % 2 == 0 and n_ma <= 8 and n_row % 2 == 0
    whole = half_lat % n_ma == 0 and lat % 16 == 0 and lat <= 64 and levels == 4
    return tiles and whole and n_row > 2 and n_ma > 1


def step(velocity, vorticity, legendre, pair_order, lat_weight, diffusivity):
    chosen = fused if fits(velocity, legendre) else local
    return chosen(velocity, vorticity, legendre, pair_order, lat_weight, diffusivity)


def solution(mesh):
    in_specs = (
        P(None, None, "row", "ma", None),
        P(None, None, "row", "ma", None),
        P("ma", None, None),
        P("ma"),
        P(),
        P(),
    )
    out_specs = P(None, None, "row", "ma", None)
    return jax.shard_map(step, mesh=mesh, in_specs=in_specs, out_specs=out_specs, check_vma=False)
```

```python
import functools
import math

import jax
import jax.numpy as jnp
import numpy as np
from jax import lax
from jax.experimental import pallas as pl
from jax.experimental.pallas import tpu as pltpu
from jax.sharding import PartitionSpec as P

NLON = 2048


STEP_SIZE = 1.0


def with_halo(cells, sides, width):
    for axis, dim in sides:
        count = lax.axis_size(axis)
        ends = count - 1
        head = lax.slice_in_dim(cells, 0, width, axis=dim)
        tail = lax.slice_in_dim(cells, cells.shape[dim] - width, cells.shape[dim], axis=dim)
        cells = jnp.concatenate(
            [
                lax.ppermute(tail, axis, [(i, (i + 1) % count) for i in range(ends)]),
                cells,
                lax.ppermute(head, axis, [((i + 1) % count, i) for i in range(ends)]),
            ],
            axis=dim,
        )
    return cells


def row_masks(low_order, pack_rows):
    orders_all = pack_rows - 1
    row_index = jnp.arange(pack_rows, dtype=jnp.int32)[None, :]
    low_column = low_order[:, None]
    is_lower = row_index < orders_all - low_column
    not_lower = jnp.logical_not(is_lower)
    even_low = row_index % 2 == 0
    even_high = (row_index + low_column) % 2 == 0
    low_pair = jnp.stack([is_lower & even_low, is_lower & jnp.logical_not(even_low)])
    high_pair = jnp.stack([not_lower & even_high, not_lower & jnp.logical_not(even_high)])
    return jnp.stack([low_pair, high_pair])


def cross_product(velocity_grid, vorticity_grid):
    return jnp.stack(
        [
            velocity_grid[1] * vorticity_grid[2] - velocity_grid[2] * vorticity_grid[1],
            velocity_grid[2] * vorticity_grid[0] - velocity_grid[0] * vorticity_grid[2],
            velocity_grid[0] * vorticity_grid[1] - velocity_grid[1] * vorticity_grid[0],
        ]
    )


def lon_table(column_order, is_imag, lon_start, lon_count):
    lon_index = lon_start + jnp.arange(lon_count, dtype=jnp.int32)
    angle_index = column_order[:, None] * lon_index[None, :] % NLON
    angle_value = angle_index.astype(jnp.float32) * (2.0 * math.pi / NLON)
    return jnp.where(is_imag[:, None], -jnp.sin(angle_value), jnp.cos(angle_value))


def local(velocity, vorticity, legendre, pair_order, lat_weight, diffusivity):
    pair_count = pair_order.shape[0]
    pack_rows = legendre.shape[1]
    half_lat = legendre.shape[2]
    nlat_all = 2 * half_lat
    levels_dev = velocity.shape[2]
    orders_all = pack_rows - 1
    inv_orders = 1.0 / math.sqrt(orders_all)
    inv_lon = 1.0 / math.sqrt(NLON)
    lon_width = NLON // 4
    mask_bool = row_masks(pair_order, pack_rows)
    fields = jnp.concatenate([velocity, vorticity], axis=0)
    masked = fields[None, None] * mask_bool.astype(jnp.bfloat16)[:, :, None, None, None]
    halves = jnp.einsum(
        "oqfilsr,srj->qfliosj", masked, legendre, preferred_element_type=jnp.float32
    )
    north_part = halves[0] + halves[1]
    south_part = halves[0] - halves[1]
    both_parts = jnp.concatenate([north_part, south_part], axis=-1)
    spectral = jnp.transpose(both_parts, (0, 1, 5, 2, 3, 4))
    spectral = spectral.reshape(6, levels_dev, nlat_all, 4 * pair_count).astype(jnp.bfloat16)
    gathered_ids = lax.all_gather(pair_order, "ma", axis=0, tiled=True)
    pair_slots = gathered_ids.reshape(-1, 1, 1, pair_count)
    both_orders = jnp.concatenate([pair_slots, orders_all - 1 - pair_slots], axis=2)
    full_shape = (both_orders.shape[0], 2, 2, pair_count)
    column_order = jnp.broadcast_to(both_orders, full_shape).reshape(-1)
    part_index = jnp.arange(2, dtype=jnp.int32)[None, :, None, None]
    is_imag = jnp.broadcast_to(part_index, full_shape).reshape(-1) == 1
    tables = [
        lon_table(column_order, is_imag, lon_block * lon_width, lon_width).astype(jnp.bfloat16)
        for lon_block in range(4)
    ]
    spec_block = lax.all_to_all(spectral, "ma", split_axis=2, concat_axis=3, tiled=True)
    accumulated = jnp.zeros((3,) + spec_block.shape[1:], jnp.float32)
    for lon_block in range(4):
        table_block = tables[lon_block]
        grid_values = (
            jnp.einsum("flac,cb->flab", spec_block, table_block, preferred_element_type=jnp.float32)
            * inv_orders
        )
        lamb_vector = cross_product(grid_values[:3], grid_values[3:])
        accumulated = accumulated + jnp.einsum(
            "flab,cb->flac",
            lamb_vector,
            table_block.astype(jnp.float32),
            precision=lax.Precision.HIGH,
            preferred_element_type=jnp.float32,
        )
    lamb_spec = (accumulated * inv_lon).astype(jnp.bfloat16)
    selector = jnp.transpose(mask_bool.astype(jnp.float32), (1, 0, 2, 3))[:, None, None, None]
    lamb_block = lax.all_to_all(lamb_spec, "ma", split_axis=3, concat_axis=2, tiled=True)
    item_count = lamb_block.shape[0]
    shaped = lamb_block.astype(jnp.float32).reshape(
        item_count, levels_dev, nlat_all, 2, 2, pair_count
    )
    shaped = jnp.transpose(shaped, (0, 1, 3, 4, 5, 2))
    north_side = shaped[..., :half_lat]
    south_side = shaped[..., half_lat:]
    weighted = jnp.stack(
        [lat_weight * (north_side + south_side), lat_weight * (north_side - south_side)]
    )
    weighted = weighted.astype(jnp.bfloat16)
    projected = jnp.einsum(
        "qfliosj,srj->qfliosr", weighted, legendre, preferred_element_type=jnp.float32
    )
    picked = jnp.sum(projected * selector, axis=(0, 4))
    tendency = jnp.transpose(picked, (0, 2, 1, 3, 4))
    source = velocity.astype(jnp.float32) + STEP_SIZE * tendency
    row_start = lax.axis_index("row") * levels_dev
    level_total = levels_dev * lax.axis_size("row")
    extended = with_halo(source.astype(jnp.bfloat16), (("row", 2),), 2).astype(source.dtype)
    padded_coupling = jnp.pad(diffusivity, (2, 2))
    wide_coupling = lax.dynamic_slice_in_dim(padded_coupling, row_start, levels_dev + 4)[
        None, None, :, None, None
    ]
    inner_coupling = wide_coupling[:, :, 1:-1]
    first_wide = (
        extended[:, :, 1:-1] + inner_coupling * (extended[:, :, :-2] + extended[:, :, 2:])
    ) / (1.0 + 2.0 * inner_coupling)
    global_level = row_start - 1 + jnp.arange(levels_dev + 2, dtype=jnp.int32)
    inside = ((global_level >= 0) & (global_level < level_total)).astype(jnp.float32)
    first_wide = first_wide * inside[None, None, :, None, None]
    own_coupling = wide_coupling[:, :, 2:-2]
    return (source + own_coupling * (first_wide[:, :, :-2] + first_wide[:, :, 2:])) / (
        1.0 + 2.0 * own_coupling
    )

def lon_count(orders_all):
    need = 3 * (orders_all - 1) + 1
    return min(NLON, -(-need // 128) * 128)


def remote(src, dst, send_sem, recv_sem, device_id):
    return pltpu.make_async_remote_copy(
        src_ref=src,
        dst_ref=dst,
        send_sem=send_sem,
        recv_sem=recv_sem,
        device_id=device_id,
        device_id_type=pl.DeviceIdType.MESH,
    )


def fused_kernel(
    n_ma, n_row, pairs, rows, levels, scale,
    velocity_ref, vorticity_ref, legendre_ref, order_ref, weight_ref, dif_ref, tab_ref, tab_t_ref,
    out_ref,
    leg_ref, rest_ref, coef_all, leg_all, rest_all, rest_t, onehot, spec, wgt, part, part_in, ext,
    coef_send, coef_recv, leg_send, leg_recv, swap_send, swap_recv, rest_send, rest_recv, part_send, part_recv, halo_send, halo_recv,
):
    me = lax.axis_index("ma")
    row = lax.axis_index("row")
    _, chunks, groups, wide_lanes = coef_all.shape
    coef_ref = coef_all.at[0]
    lanes = (chunks + 1) * wide_lanes
    fields2 = groups // 2
    orders = rows - 1
    slots = 2 * pairs
    lat = leg_ref.shape[2]
    main = pairs * orders
    f32 = jnp.float32
    bf16 = jnp.bfloat16
    n_z = n_ma // 2
    z, y = me // 2, lax.rem(me, 2)
    mate = me + 1 - 2 * y
    half = lax.rem(row, 2)
    mate_row = row + 1 - 2 * half

    def target(s):
        return lax.rem(z + s // 2, n_z) * 2 + lax.rem(y + lax.rem(s, 2), 2)

    def origin(s):
        return lax.rem(z + n_z - s // 2, n_z) * 2 + lax.rem(y + lax.rem(s, 2), 2)

    left = lax.rem(row + n_row - 1, n_row)
    right = lax.rem(row + 1, n_row)

    barrier = pltpu.get_barrier_semaphore()
    for d in range(1, n_ma):
        pl.semaphore_signal(
            barrier, inc=1, device_id=(lax.rem(me + d, n_ma), row), device_id_type=pl.DeviceIdType.MESH
        )
    for side in (left, right):
        pl.semaphore_signal(barrier, inc=1, device_id=(me, side), device_id_type=pl.DeviceIdType.MESH)

    per_chunk = pairs // chunks
    packs = [
        jnp.concatenate([velocity_ref[...].astype(f32)[:, p], vorticity_ref[...].astype(f32)[:, p]], axis=0)
        for p in range(pairs)
    ]
    square = (wide_lanes, wide_lanes)
    column = lax.broadcasted_iota(jnp.int32, (groups, wide_lanes), 1)
    ends = jnp.zeros((groups, wide_lanes), f32)
    for p in range(pairs):
        ends = jnp.where(column == p, packs[p][:, orders:], ends)
    ends = jnp.concatenate([ends, jnp.zeros((wide_lanes - groups, wide_lanes), f32)], axis=0)
    ends = jnp.transpose(ends)[0:pairs, 0 : wide_lanes // 2]
    tails = []
    for c in range(chunks):
        members = range(c * per_chunk, (c + 1) * per_chunk)
        coef_all[0, c] = jnp.concatenate([packs[p][:, :orders] for p in members], axis=1).astype(bf16)
        tables = [legendre_ref[p].astype(f32) for p in members]
        turned = jnp.transpose(jnp.concatenate([t[:orders] for t in tables], axis=0)).astype(bf16)
        for b in range(n_ma):
            leg_ref[b, c] = turned[b * lat : (b + 1) * lat]
        tails += [t[orders:] for t in tables]
    tails = jnp.concatenate(tails, axis=0)
    order_rows = [jnp.full((1, wide_lanes), order_ref[p].astype(f32)) for p in range(pairs)]
    filler = jnp.zeros((pairs, wide_lanes // 2 - lat), f32)
    for b in range(n_ma):
        data_rows = jnp.concatenate([ends, tails[:, b * lat : (b + 1) * lat], filler], axis=1)
        rest_ref[b] = jnp.concatenate([data_rows] + order_rows, axis=0).astype(bf16)
    weight = jnp.zeros((1, lat), f32)
    for b in range(n_ma):
        weight = jnp.where(me == b, weight_ref[:, b * lat : (b + 1) * lat], weight)
    weight = weight * scale

    pl.semaphore_wait(barrier, n_ma + 1)

    def coef_copy(s):
        if s % 2 == 0:
            return remote(coef_ref, coef_all.at[s], coef_send.at[s], coef_recv.at[s], (target(s), row))
        src = coef_ref if s == 1 else coef_all.at[s - 1]
        return remote(src, coef_all.at[s], coef_send.at[s], coef_recv.at[s], (mate, row))

    def leg_copy(s):
        peer = target(s)
        return remote(
            leg_ref.at[peer, half], leg_all.at[s, half], leg_send.at[s], leg_recv.at[s], (peer, row)
        )

    def swap_copy(s):
        return remote(
            leg_all.at[s, half], leg_all.at[s, half], swap_send.at[s], swap_recv.at[s], (me, mate_row)
        )

    def rest_copy(s):
        peer = target(s)
        return remote(rest_ref.at[peer], rest_all.at[s], rest_send.at[s], rest_recv.at[s], (peer, row))

    for s in range(1, n_ma):
        rest_copy(s).start()
    for s in range(n_ma - 2, 0, -2):
        coef_copy(s).start()
        leg_copy(s).start()
        leg_copy(s + 1).start()
    coef_copy(1).start()
    leg_copy(1).start()

    leg_all[0] = leg_ref[me]
    rest_all[0] = rest_ref[me]

    lane = lax.broadcasted_iota(jnp.int32, (slots, lanes), 1)
    sub = lax.broadcasted_iota(jnp.int32, (slots, lanes), 0)
    is_high = (sub % 2) == 1
    m_lane = lax.broadcasted_iota(jnp.int32, (slots, orders), 1)
    m_sub = lax.broadcasted_iota(jnp.int32, (slots, orders), 0)

    def lows(d):
        tile = rest_all[d].astype(jnp.float32)
        return [tile[pairs + p : pairs + p + 1, 0:1].astype(jnp.int32) for p in range(pairs)]

    def masks(d):
        values = lows(d)
        extra = lane - main - 8 * d
        in_main = lane < main
        lane_pair = jnp.where(in_main, lane // orders, extra)
        lane_row = jnp.where(in_main, lane % orders, orders)
        own = lane_pair == sub // 2
        low = jnp.zeros((slots, lanes), jnp.int32)
        for p in range(pairs):
            low = jnp.where(lane_pair == p, values[p], low)
        lower = lane_row < orders - low
        picked = own & jnp.logical_xor(is_high, lower)
        parity = jnp.where(is_high, lane_row + low, lane_row) & 1
        even = (picked & (parity == 0)).astype(f32)
        odd = (picked & (parity == 1)).astype(f32)
        return even, odd

    def leg_of(d):
        tail = rest_t[wide_lanes // 2 : wide_lanes // 2 + lat, :].astype(bf16)
        return jnp.concatenate([leg_all[d, c] for c in range(chunks)] + [tail], axis=1)

    def synth(d, carry):
        values = lows(d)
        order = jnp.zeros((slots, orders), jnp.int32)
        for p in range(pairs):
            order = jnp.where(m_sub == 2 * p, values[p], order)
            order = jnp.where(m_sub == 2 * p + 1, orders - 1 - values[p], order)
        base = pl.multiple_of(d * slots, slots)
        onehot[pl.ds(base, slots), :] = (m_lane == order).astype(f32)
        even, odd = masks(d)
        coef = jnp.concatenate(
            [coef_all[d, c].astype(f32) for c in range(chunks)] + [rest_t[0:groups, :]], axis=1
        )
        leg = leg_of(d)
        for h in range(2):
            mask = even + odd if h == 0 else even - odd
            lhs = (coef[:, None, :] * mask[None]).reshape(groups * slots, lanes).astype(bf16)
            made = lax.dot_general(lhs, leg, (((1,), (1,)), ((), ())), preferred_element_type=f32)
            spec[h, :, pl.ds(base, slots), :] = made.reshape(groups, slots, lat)
        return carry

    for s in range(1, n_ma):
        rest_copy(s).wait_recv()
    rest = rest_all[...].astype(f32).reshape(n_ma * 8, wide_lanes)
    rest = jnp.concatenate([rest, jnp.zeros((wide_lanes - n_ma * 8, wide_lanes), f32)], axis=0)
    rest_t[...] = jnp.transpose(rest)
    leg_copy(1).wait_recv()
    swap_copy(1).start()
    for s in range(2, n_ma, 2):
        coef_copy(s).wait_recv()
        coef_copy(s + 1).start()
        for t in (s, s + 1):
            leg_copy(t).wait_recv()
            swap_copy(t).start()
    synth(0, 0)
    for s in range(1, n_ma):
        if s % 2 == 1:
            coef_copy(s).wait_recv()
        remote(
            leg_all.at[s, half], leg_all.at[s, 1 - half], swap_send.at[s], swap_recv.at[s], (me, mate_row)
        ).wait_recv()
        synth(s, 0)

    hot = onehot[...].astype(bf16)
    full = n_ma * slots
    to_grid = jnp.concatenate(
        [
            lax.dot_general(tab_t_ref[c], hot, (((1,), (1,)), ((), ())), preferred_element_type=f32)
            for c in range(2)
        ],
        axis=1,
    ).astype(bf16)
    to_spec = jnp.concatenate(
        [jnp.dot(hot, tab_ref[c], preferred_element_type=f32) for c in range(2)], axis=0
    ).astype(bf16)

    def middle(k, carry):
        halves = []
        for h in range(2):
            grids = []
            for g in range(2):
                for f in range(3):
                    at = (g * 3 + f) * 2 * levels + k
                    block = jnp.concatenate([spec[h, at], spec[h, at + levels]], axis=0).astype(bf16)
                    grids.append(jnp.dot(to_grid, block, preferred_element_type=f32))
            u, w = grids[:3], grids[3:]
            lamb = [
                u[1] * w[2] - u[2] * w[1],
                u[2] * w[0] - u[0] * w[2],
                u[0] * w[1] - u[1] * w[0],
            ]
            halves.append(
                [jnp.dot(to_spec, x.astype(bf16), preferred_element_type=f32) for x in lamb]
            )
        for f in range(3):
            north, south = halves[0][f], halves[1][f]
            for q, mixed in enumerate((weight * (north + south), weight * (north - south))):
                for c in range(2):
                    wgt[q, (f * 2 + c) * levels + k] = mixed[c * full : (c + 1) * full]
        return carry

    lax.fori_loop(0, levels, middle, 0)

    def part_copy(d):
        return remote(part.at[d], part_in.at[d], part_send.at[d], part_recv.at[d], (origin(d), row))

    def analyse(d):
        base = pl.multiple_of(d * slots, slots)
        total = None
        for q, mask in enumerate(masks(d)):
            lhs = wgt[q, :, pl.ds(base, slots), :].reshape(fields2 * slots, lat).astype(bf16)
            made = jnp.dot(lhs, leg_of(d), preferred_element_type=f32)
            made = made.reshape(fields2, slots, lanes) * mask[None]
            total = made if total is None else total + made
        return jnp.sum(total, axis=1)

    def project(i, carry):
        d = n_ma - i
        part[d] = analyse(d).astype(bf16)
        part_copy(d).start()
        return carry

    lax.fori_loop(1, n_ma, project, 0)
    source = analyse(0)

    def gather(i, total):
        d = n_ma - i
        part_copy(d).wait_recv()
        return total + part_in[d].astype(f32)

    source = lax.fori_loop(1, n_ma, gather, source)
    tail = source[:, main:]
    for shift in (8, 16, 32):
        tail = tail + pltpu.roll(tail, wide_lanes - shift, 1)
    own_tail = rest_t[0:fields2, :]
    heads = [source[:, c * wide_lanes : (c + 1) * wide_lanes] + coef_ref[c, 0:fields2].astype(f32) for c in range(chunks)]
    source = jnp.concatenate(heads + [tail + own_tail], axis=1)
    source = source.reshape(fields2 // levels, levels, lanes)
    for k in range(levels):
        ext[k + 2] = source[:, k, :]
    to_left = remote(ext.at[2:4], ext.at[levels + 2 : levels + 4], halo_send.at[0], halo_recv.at[0], (me, left))
    to_right = remote(ext.at[levels : levels + 2], ext.at[0:2], halo_send.at[1], halo_recv.at[1], (me, right))
    to_left.start()
    to_right.start()

    for s in range(1, n_ma):
        coef_copy(s).wait_send()
        leg_copy(s).wait_send()
        swap_copy(s).wait_send()
        rest_copy(s).wait_send()
        part_copy(s).wait_send()
    to_left.wait()
    to_right.wait()

    shape = (fields2 // levels, lanes)
    has_left = (row > 0).astype(f32)
    has_right = (row < n_row - 1).astype(f32)
    wide = [ext[i] for i in range(levels + 4)]
    for i in range(2):
        wide[i] = wide[i] * has_left
        wide[levels + 2 + i] = wide[levels + 2 + i] * has_right
    coupling = [jnp.full(shape, dif_ref[lax.rem((row + n_row) * levels + i - 2, n_row * levels)]) for i in range(levels + 4)]
    inverse = [1.0 / (1.0 + 2.0 * c) for c in coupling]
    first = [
        (wide[i] + coupling[i] * (wide[i - 1] + wide[i + 1])) * inverse[i] for i in range(1, levels + 3)
    ]
    first[0] = first[0] * has_left
    first[-1] = first[-1] * has_right
    for k in range(levels):
        done = (wide[k + 2] + coupling[k + 2] * (first[k] + first[k + 2])) * inverse[k + 2]
        out_ref[k] = done[:, : main + pairs]


def fused(velocity, vorticity, legendre, pair_order, lat_weight, diffusivity):
    n_ma = lax.axis_size("ma")
    n_row = lax.axis_size("row")
    pairs, rows, half_lat = legendre.shape
    levels = velocity.shape[2]
    orders = rows - 1
    main = pairs * orders
    used = main + pairs
    chunks = main // 128
    lanes = main + 128
    lat = half_lat // n_ma
    slots = 2 * pairs
    full = n_ma * slots
    points = lon_count(orders)
    bf16 = jnp.bfloat16
    f32 = jnp.float32
    groups = 12 * levels
    scale = (NLON / points) / math.sqrt(NLON) / orders
    angle = np.outer(np.arange(orders), np.arange(points)) % points * (2.0 * math.pi / points)
    table = np.stack([np.cos(angle), -np.sin(angle)])
    tab = jnp.asarray(table, bf16)
    tab_t = jnp.asarray(np.transpose(table, (0, 2, 1)), bf16)
    vmem = pl.BlockSpec(memory_space=pltpu.VMEM)
    smem = pl.BlockSpec(memory_space=pltpu.SMEM)
    out = pl.pallas_call(
        functools.partial(fused_kernel, n_ma, n_row, pairs, rows, levels, scale),
        out_shape=jax.ShapeDtypeStruct((levels, 6, used), f32),
        in_specs=[vmem, vmem, vmem, smem, vmem, smem, vmem, vmem],
        out_specs=vmem,
        scratch_shapes=[
            pltpu.VMEM((n_ma, chunks, lat, 128), bf16),
            pltpu.VMEM((n_ma, 8, 128), bf16),
            pltpu.VMEM((n_ma, chunks, groups, 128), bf16),
            pltpu.VMEM((n_ma, chunks, lat, 128), bf16),
            pltpu.VMEM((n_ma, 8, 128), bf16),
            pltpu.VMEM((128, 128), f32),
            pltpu.VMEM((full, orders), f32),
            pltpu.VMEM((2, groups, full, lat), f32),
            pltpu.VMEM((2, groups // 2, full, lat), f32),
            pltpu.VMEM((n_ma, groups // 2, lanes), bf16),
            pltpu.VMEM((n_ma, groups // 2, lanes), bf16),
            pltpu.VMEM((levels + 4, 6, lanes), f32),
        ]
        + [pltpu.SemaphoreType.DMA((n_ma,))] * 10
        + [pltpu.SemaphoreType.DMA((2,))] * 2,
        compiler_params=pltpu.CompilerParams(
            collective_id=0, has_side_effects=True, vmem_limit_bytes=48 * 1024 * 1024
        ),
    )(
        velocity.reshape(6 * levels, pairs, rows),
        vorticity.reshape(6 * levels, pairs, rows),
        legendre,
        pair_order,
        lat_weight[None],
        diffusivity,
        tab,
        tab_t,
    )
    out = jnp.concatenate(
        [out[..., :main].reshape(levels, 6, pairs, orders), out[..., main:, None]], axis=3
    )
    return jnp.transpose(out.reshape(levels, 3, 2, pairs, rows), (1, 2, 0, 3, 4))


def fits(velocity, legendre):
    n_ma = lax.axis_size("ma")
    n_row = lax.axis_size("row")
    pairs, rows, half_lat = legendre.shape
    levels = velocity.shape[2]
    lat = half_lat // n_ma
    tiles = pairs == 4 and pairs * (rows - 1) == 256 and n_ma % 2 == 0 and n_ma <= 8 and n_row % 2 == 0
    whole = half_lat % n_ma == 0 and lat % 16 == 0 and lat <= 64 and levels == 4
    return tiles and whole and n_row > 2 and n_ma > 1


def step(velocity, vorticity, legendre, pair_order, lat_weight, diffusivity):
    chosen = fused if fits(velocity, legendre) else local
    return chosen(velocity, vorticity, legendre, pair_order, lat_weight, diffusivity)


def solution(mesh):
    in_specs = (
        P(None, None, "row", "ma", None),
        P(None, None, "row", "ma", None),
        P("ma", None, None),
        P("ma"),
        P(),
        P(),
    )
    out_specs = P(None, None, "row", "ma", None)
    return jax.shard_map(step, mesh=mesh, in_specs=in_specs, out_specs=out_specs, check_vma=False)
```

```python
import functools
import math

import jax
import jax.numpy as jnp
import numpy as np
from jax import lax
from jax.experimental import pallas as pl
from jax.experimental.pallas import tpu as pltpu
from jax.sharding import PartitionSpec as P

NLON = 2048


STEP_SIZE = 1.0


def with_halo(cells, sides, width):
    for axis, dim in sides:
        count = lax.axis_size(axis)
        ends = count - 1
        head = lax.slice_in_dim(cells, 0, width, axis=dim)
        tail = lax.slice_in_dim(cells, cells.shape[dim] - width, cells.shape[dim], axis=dim)
        cells = jnp.concatenate(
            [
                lax.ppermute(tail, axis, [(i, (i + 1) % count) for i in range(ends)]),
                cells,
                lax.ppermute(head, axis, [((i + 1) % count, i) for i in range(ends)]),
            ],
            axis=dim,
        )
    return cells


def row_masks(low_order, pack_rows):
    orders_all = pack_rows - 1
    row_index = jnp.arange(pack_rows, dtype=jnp.int32)[None, :]
    low_column = low_order[:, None]
    is_lower = row_index < orders_all - low_column
    not_lower = jnp.logical_not(is_lower)
    even_low = row_index % 2 == 0
    even_high = (row_index + low_column) % 2 == 0
    low_pair = jnp.stack([is_lower & even_low, is_lower & jnp.logical_not(even_low)])
    high_pair = jnp.stack([not_lower & even_high, not_lower & jnp.logical_not(even_high)])
    return jnp.stack([low_pair, high_pair])


def cross_product(velocity_grid, vorticity_grid):
    return jnp.stack(
        [
            velocity_grid[1] * vorticity_grid[2] - velocity_grid[2] * vorticity_grid[1],
            velocity_grid[2] * vorticity_grid[0] - velocity_grid[0] * vorticity_grid[2],
            velocity_grid[0] * vorticity_grid[1] - velocity_grid[1] * vorticity_grid[0],
        ]
    )


def lon_table(column_order, is_imag, lon_start, lon_count):
    lon_index = lon_start + jnp.arange(lon_count, dtype=jnp.int32)
    angle_index = column_order[:, None] * lon_index[None, :] % NLON
    angle_value = angle_index.astype(jnp.float32) * (2.0 * math.pi / NLON)
    return jnp.where(is_imag[:, None], -jnp.sin(angle_value), jnp.cos(angle_value))


def local(velocity, vorticity, legendre, pair_order, lat_weight, diffusivity):
    pair_count = pair_order.shape[0]
    pack_rows = legendre.shape[1]
    half_lat = legendre.shape[2]
    nlat_all = 2 * half_lat
    levels_dev = velocity.shape[2]
    orders_all = pack_rows - 1
    inv_orders = 1.0 / math.sqrt(orders_all)
    inv_lon = 1.0 / math.sqrt(NLON)
    lon_width = NLON // 4
    mask_bool = row_masks(pair_order, pack_rows)
    fields = jnp.concatenate([velocity, vorticity], axis=0)
    masked = fields[None, None] * mask_bool.astype(jnp.bfloat16)[:, :, None, None, None]
    halves = jnp.einsum(
        "oqfilsr,srj->qfliosj", masked, legendre, preferred_element_type=jnp.float32
    )
    north_part = halves[0] + halves[1]
    south_part = halves[0] - halves[1]
    both_parts = jnp.concatenate([north_part, south_part], axis=-1)
    spectral = jnp.transpose(both_parts, (0, 1, 5, 2, 3, 4))
    spectral = spectral.reshape(6, levels_dev, nlat_all, 4 * pair_count).astype(jnp.bfloat16)
    gathered_ids = lax.all_gather(pair_order, "ma", axis=0, tiled=True)
    pair_slots = gathered_ids.reshape(-1, 1, 1, pair_count)
    both_orders = jnp.concatenate([pair_slots, orders_all - 1 - pair_slots], axis=2)
    full_shape = (both_orders.shape[0], 2, 2, pair_count)
    column_order = jnp.broadcast_to(both_orders, full_shape).reshape(-1)
    part_index = jnp.arange(2, dtype=jnp.int32)[None, :, None, None]
    is_imag = jnp.broadcast_to(part_index, full_shape).reshape(-1) == 1
    tables = [
        lon_table(column_order, is_imag, lon_block * lon_width, lon_width).astype(jnp.bfloat16)
        for lon_block in range(4)
    ]
    spec_block = lax.all_to_all(spectral, "ma", split_axis=2, concat_axis=3, tiled=True)
    accumulated = jnp.zeros((3,) + spec_block.shape[1:], jnp.float32)
    for lon_block in range(4):
        table_block = tables[lon_block]
        grid_values = (
            jnp.einsum("flac,cb->flab", spec_block, table_block, preferred_element_type=jnp.float32)
            * inv_orders
        )
        lamb_vector = cross_product(grid_values[:3], grid_values[3:])
        accumulated = accumulated + jnp.einsum(
            "flab,cb->flac",
            lamb_vector,
            table_block.astype(jnp.float32),
            precision=lax.Precision.HIGH,
            preferred_element_type=jnp.float32,
        )
    lamb_spec = (accumulated * inv_lon).astype(jnp.bfloat16)
    selector = jnp.transpose(mask_bool.astype(jnp.float32), (1, 0, 2, 3))[:, None, None, None]
    lamb_block = lax.all_to_all(lamb_spec, "ma", split_axis=3, concat_axis=2, tiled=True)
    item_count = lamb_block.shape[0]
    shaped = lamb_block.astype(jnp.float32).reshape(
        item_count, levels_dev, nlat_all, 2, 2, pair_count
    )
    shaped = jnp.transpose(shaped, (0, 1, 3, 4, 5, 2))
    north_side = shaped[..., :half_lat]
    south_side = shaped[..., half_lat:]
    weighted = jnp.stack(
        [lat_weight * (north_side + south_side), lat_weight * (north_side - south_side)]
    )
    weighted = weighted.astype(jnp.bfloat16)
    projected = jnp.einsum(
        "qfliosj,srj->qfliosr", weighted, legendre, preferred_element_type=jnp.float32
    )
    picked = jnp.sum(projected * selector, axis=(0, 4))
    tendency = jnp.transpose(picked, (0, 2, 1, 3, 4))
    source = velocity.astype(jnp.float32) + STEP_SIZE * tendency
    row_start = lax.axis_index("row") * levels_dev
    level_total = levels_dev * lax.axis_size("row")
    extended = with_halo(source.astype(jnp.bfloat16), (("row", 2),), 2).astype(source.dtype)
    padded_coupling = jnp.pad(diffusivity, (2, 2))
    wide_coupling = lax.dynamic_slice_in_dim(padded_coupling, row_start, levels_dev + 4)[
        None, None, :, None, None
    ]
    inner_coupling = wide_coupling[:, :, 1:-1]
    first_wide = (
        extended[:, :, 1:-1] + inner_coupling * (extended[:, :, :-2] + extended[:, :, 2:])
    ) / (1.0 + 2.0 * inner_coupling)
    global_level = row_start - 1 + jnp.arange(levels_dev + 2, dtype=jnp.int32)
    inside = ((global_level >= 0) & (global_level < level_total)).astype(jnp.float32)
    first_wide = first_wide * inside[None, None, :, None, None]
    own_coupling = wide_coupling[:, :, 2:-2]
    return (source + own_coupling * (first_wide[:, :, :-2] + first_wide[:, :, 2:])) / (
        1.0 + 2.0 * own_coupling
    )

def lon_count(orders_all):
    need = 3 * (orders_all - 1) + 1
    return min(NLON, -(-need // 128) * 128)


def remote(src, dst, send_sem, recv_sem, device_id):
    return pltpu.make_async_remote_copy(
        src_ref=src,
        dst_ref=dst,
        send_sem=send_sem,
        recv_sem=recv_sem,
        device_id=device_id,
        device_id_type=pl.DeviceIdType.MESH,
    )


def fused_kernel(
    n_ma, n_row, pairs, rows, levels, scale,
    velocity_ref, vorticity_ref, legendre_ref, order_ref, weight_ref, dif_ref, tab_ref, tab_t_ref,
    out_ref,
    leg_ref, rest_ref, coef_all, leg_all, rest_all, rest_t, spec, wgt, part, part_in, ext,
    coef_send, coef_recv, leg_send, leg_recv, swap_send, swap_recv, rest_send, rest_recv, part_send, part_recv, halo_send, halo_recv,
):
    me = lax.axis_index("ma")
    row = lax.axis_index("row")
    _, chunks, groups, wide_lanes = coef_all.shape
    coef_ref = coef_all.at[0]
    lanes = (chunks + 1) * wide_lanes
    fields2 = groups // 2
    orders = rows - 1
    slots = 2 * pairs
    lat = leg_ref.shape[2]
    main = pairs * orders
    f32 = jnp.float32
    bf16 = jnp.bfloat16
    n_z = n_ma // 2
    z, y = me // 2, lax.rem(me, 2)
    mate = me + 1 - 2 * y
    half = lax.rem(row, 2)
    mate_row = row + 1 - 2 * half

    def target(s):
        return lax.rem(z + s // 2, n_z) * 2 + lax.rem(y + lax.rem(s, 2), 2)

    def origin(s):
        return lax.rem(z + n_z - s // 2, n_z) * 2 + lax.rem(y + lax.rem(s, 2), 2)

    left = lax.rem(row + n_row - 1, n_row)
    right = lax.rem(row + 1, n_row)

    barrier = pltpu.get_barrier_semaphore()
    for d in range(1, n_ma):
        pl.semaphore_signal(
            barrier, inc=1, device_id=(lax.rem(me + d, n_ma), row), device_id_type=pl.DeviceIdType.MESH
        )
    for side in (left, right):
        pl.semaphore_signal(barrier, inc=1, device_id=(me, side), device_id_type=pl.DeviceIdType.MESH)

    per_chunk = pairs // chunks
    packs = [
        jnp.concatenate([velocity_ref[...].astype(f32)[:, p], vorticity_ref[...].astype(f32)[:, p]], axis=0)
        for p in range(pairs)
    ]
    square = (wide_lanes, wide_lanes)
    column = lax.broadcasted_iota(jnp.int32, (groups, wide_lanes), 1)
    ends = jnp.zeros((groups, wide_lanes), f32)
    for p in range(pairs):
        ends = jnp.where(column == p, packs[p][:, orders:], ends)
    ends = jnp.concatenate([ends, jnp.zeros((wide_lanes - groups, wide_lanes), f32)], axis=0)
    ends = jnp.transpose(ends)[0:pairs, 0 : wide_lanes // 2]
    tails = []
    all_tables = legendre_ref[...].astype(f32)
    for c in range(chunks):
        members = range(c * per_chunk, (c + 1) * per_chunk)
        coef_all[0, c] = jnp.concatenate([packs[p][:, :orders] for p in members], axis=1).astype(bf16)
        tables = [all_tables[:, p] for p in members]
        turned = jnp.transpose(jnp.concatenate([t[:orders] for t in tables], axis=0)).astype(bf16)
        for b in range(n_ma):
            leg_ref[b, c] = turned[b * lat : (b + 1) * lat]
        tails += [t[orders:] for t in tables]
    tails = jnp.concatenate(tails, axis=0)
    order_rows = [jnp.full((1, wide_lanes), order_ref[p].astype(f32)) for p in range(pairs)]
    filler = jnp.zeros((pairs, wide_lanes // 2 - lat), f32)
    for b in range(n_ma):
        data_rows = jnp.concatenate([ends, tails[:, b * lat : (b + 1) * lat], filler], axis=1)
        rest_ref[b] = jnp.concatenate([data_rows] + order_rows, axis=0).astype(bf16)
    weight = jnp.zeros((1, lat), f32)
    all_weights = weight_ref[...].reshape(1, n_ma * lat)
    for b in range(n_ma):
        weight = jnp.where(me == b, all_weights[:, b * lat : (b + 1) * lat], weight)
    weight = jnp.concatenate([weight, weight], axis=1) * scale

    pl.semaphore_wait(barrier, n_ma + 1)

    def coef_copy(s):
        if s % 2 == 0:
            return remote(coef_ref, coef_all.at[s], coef_send.at[s], coef_recv.at[s], (target(s), row))
        src = coef_ref if s == 1 else coef_all.at[s - 1]
        return remote(src, coef_all.at[s], coef_send.at[s], coef_recv.at[s], (mate, row))

    def leg_copy(s):
        peer = target(s)
        return remote(
            leg_ref.at[peer, half], leg_all.at[s, half], leg_send.at[s], leg_recv.at[s], (peer, row)
        )

    def swap_copy(s):
        return remote(
            leg_all.at[s, half], leg_all.at[s, half], swap_send.at[s], swap_recv.at[s], (me, mate_row)
        )

    def rest_copy(s):
        peer = target(s)
        return remote(rest_ref.at[peer], rest_all.at[s], rest_send.at[s], rest_recv.at[s], (peer, row))

    for s in range(1, n_ma):
        rest_copy(s).start()
    for s in range(n_ma - 2, 0, -2):
        coef_copy(s).start()
        leg_copy(s).start()
        leg_copy(s + 1).start()
    coef_copy(1).start()
    leg_copy(1).start()

    leg_all[0] = leg_ref[me]
    rest_all[0] = rest_ref[me]

    lane = lax.broadcasted_iota(jnp.int32, (slots, lanes), 1)
    sub = lax.broadcasted_iota(jnp.int32, (slots, lanes), 0)
    is_high = (sub % 2) == 1
    m_lane = lax.broadcasted_iota(jnp.int32, (slots, orders), 1)
    m_sub = lax.broadcasted_iota(jnp.int32, (slots, orders), 0)

    def lows(d):
        tile = rest_all[d].astype(jnp.float32)
        return [tile[pairs + p : pairs + p + 1, 0:1].astype(jnp.int32) for p in range(pairs)]

    def masks(d):
        values = lows(d)
        extra = lane - main - 8 * d
        in_main = lane < main
        lane_pair = jnp.where(in_main, lane // orders, extra)
        lane_row = jnp.where(in_main, lane % orders, orders)
        own = lane_pair == sub // 2
        low = jnp.zeros((slots, lanes), jnp.int32)
        for p in range(pairs):
            low = jnp.where(lane_pair == p, values[p], low)
        lower = lane_row < orders - low
        picked = own & jnp.logical_xor(is_high, lower)
        parity = jnp.where(is_high, lane_row + low, lane_row) & 1
        even = (picked & (parity == 0)).astype(f32)
        odd = (picked & (parity == 1)).astype(f32)
        return even, odd

    def leg_of(d):
        tail = rest_t[wide_lanes // 2 : wide_lanes // 2 + lat, :].astype(bf16)
        return jnp.concatenate([leg_all[d, c] for c in range(chunks)] + [tail], axis=1)

    def place(d):
        values = lows(d)
        order = jnp.zeros((slots, orders), jnp.int32)
        for p in range(pairs):
            order = jnp.where(m_sub == 2 * p, values[p], order)
            order = jnp.where(m_sub == 2 * p + 1, orders - 1 - values[p], order)
        return (m_lane == order).astype(f32)

    def both(leg):
        return jnp.concatenate([leg, leg], axis=0), jnp.concatenate([leg, -leg], axis=0)

    def synth(d):
        even, odd = masks(d)
        coef = jnp.concatenate(
            [coef_all[d, c].astype(f32) for c in range(chunks)] + [rest_t[0:groups, :]], axis=1
        )
        leg = leg_of(d)
        lhs = [
            (coef[:, None, :] * mask[None]).reshape(groups * slots, lanes).astype(bf16)
            for mask in (even, odd)
        ]
        made = lax.dot_general(
            jnp.concatenate(lhs, axis=1),
            jnp.concatenate(both(leg), axis=1),
            (((1,), (1,)), ((), ())),
            preferred_element_type=f32,
        )
        spec[:, d * slots : (d + 1) * slots, :] = made.reshape(groups, slots, 2 * lat)

    full = n_ma * slots

    def grid_tables():
        hot = jnp.concatenate([place(d) for d in range(n_ma)], axis=0).astype(bf16)
        to_grid = jnp.concatenate(
            [
                lax.dot_general(tab_t_ref[c], hot, (((1,), (1,)), ((), ())), preferred_element_type=f32)
                for c in range(2)
            ],
            axis=1,
        ).astype(bf16)
        to_spec = jnp.concatenate(
            [jnp.dot(hot, tab_ref[c], preferred_element_type=f32) for c in range(2)], axis=0
        ).astype(bf16)
        return to_grid, to_spec

    for s in range(1, n_ma):
        rest_copy(s).wait_recv()
    rest = rest_all[...].astype(f32).reshape(n_ma * 8, wide_lanes)
    rest = jnp.concatenate([rest, jnp.zeros((wide_lanes - n_ma * 8, wide_lanes), f32)], axis=0)
    rest_t[...] = jnp.transpose(rest)
    leg_copy(1).wait_recv()
    swap_copy(1).start()
    for s in range(2, n_ma, 2):
        coef_copy(s).wait_recv()
        coef_copy(s + 1).start()
        for t in (s, s + 1):
            leg_copy(t).wait_recv()
            swap_copy(t).start()
        if s == 2:
            to_grid, to_spec = grid_tables()
        if s == n_ma - 4:
            synth(0)
    if n_ma < 6:
        synth(0)
    for s in range(1, n_ma):
        if s % 2 == 1:
            coef_copy(s).wait_recv()
        remote(
            leg_all.at[s, half], leg_all.at[s, 1 - half], swap_send.at[s], swap_recv.at[s], (me, mate_row)
        ).wait_recv()
        synth(s)

    def middle(k, carry):
        grids = []
        for gf in range(6):
            at = gf * 2 * levels + k
            block = jnp.concatenate([spec[at], spec[at + levels]], axis=0).astype(bf16)
            grids.append(jnp.dot(to_grid, block, preferred_element_type=f32))
        u, w = grids[:3], grids[3:]
        lamb = [
            u[1] * w[2] - u[2] * w[1],
            u[2] * w[0] - u[0] * w[2],
            u[0] * w[1] - u[1] * w[0],
        ]
        for f in range(3):
            made = weight * jnp.dot(to_spec, lamb[f].astype(bf16), preferred_element_type=f32)
            for c in range(2):
                wgt[(f * 2 + c) * levels + k] = made[c * full : (c + 1) * full]
        return carry

    lax.fori_loop(0, levels, middle, 0)

    def part_copy(d):
        return remote(part.at[d], part_in.at[d], part_send.at[d], part_recv.at[d], (origin(d), row))

    def analyse(d):
        base = pl.multiple_of(d * slots, slots)
        total = None
        lhs = wgt[:, pl.ds(base, slots), :].reshape(fields2 * slots, 2 * lat).astype(bf16)
        for leg, mask in zip(both(leg_of(d)), masks(d)):
            made = jnp.dot(lhs, leg, preferred_element_type=f32)
            made = made.reshape(fields2, slots, lanes) * mask[None]
            total = made if total is None else total + made
        return jnp.sum(total, axis=1)

    def project(i, carry):
        d = n_ma - i
        part[d] = analyse(d).astype(bf16)
        part_copy(d).start()
        return carry

    lax.fori_loop(1, n_ma, project, 0)
    source = analyse(0)

    def gather(i, total):
        d = n_ma - i
        part_copy(d).wait_recv()
        return total + part_in[d].astype(f32)

    source = lax.fori_loop(1, n_ma, gather, source)
    tail = source[:, main:]
    for shift in (8, 16, 32):
        tail = tail + pltpu.roll(tail, wide_lanes - shift, 1)
    own_tail = rest_t[0:fields2, :]
    heads = [source[:, c * wide_lanes : (c + 1) * wide_lanes] + coef_ref[c, 0:fields2].astype(f32) for c in range(chunks)]
    source = jnp.concatenate(heads + [tail + own_tail], axis=1)
    source = source.reshape(fields2 // levels, levels, lanes)
    for k in range(levels):
        ext[k + 2] = source[:, k, :]
    to_left = remote(ext.at[2:4], ext.at[levels + 2 : levels + 4], halo_send.at[0], halo_recv.at[0], (me, left))
    to_right = remote(ext.at[levels : levels + 2], ext.at[0:2], halo_send.at[1], halo_recv.at[1], (me, right))
    to_left.start()
    to_right.start()

    for s in range(1, n_ma):
        coef_copy(s).wait_send()
        leg_copy(s).wait_send()
        swap_copy(s).wait_send()
        rest_copy(s).wait_send()
        part_copy(s).wait_send()
    to_left.wait()
    to_right.wait()

    shape = (fields2 // levels, lanes)
    has_left = (row > 0).astype(f32)
    has_right = (row < n_row - 1).astype(f32)
    wide = [ext[i] for i in range(levels + 4)]
    for i in range(2):
        wide[i] = wide[i] * has_left
        wide[levels + 2 + i] = wide[levels + 2 + i] * has_right
    coupling = [jnp.full(shape, dif_ref[lax.rem((row + n_row) * levels + i - 2, n_row * levels)]) for i in range(levels + 4)]
    inverse = [1.0 / (1.0 + 2.0 * c) for c in coupling]
    first = [
        (wide[i] + coupling[i] * (wide[i - 1] + wide[i + 1])) * inverse[i] for i in range(1, levels + 3)
    ]
    first[0] = first[0] * has_left
    first[-1] = first[-1] * has_right
    for k in range(levels):
        done = (wide[k + 2] + coupling[k + 2] * (first[k] + first[k + 2])) * inverse[k + 2]
        out_ref[k] = done[:, : main + pairs]


def fused(velocity, vorticity, legendre, pair_order, lat_weight, diffusivity):
    n_ma = lax.axis_size("ma")
    n_row = lax.axis_size("row")
    pairs, rows, half_lat = legendre.shape
    levels = velocity.shape[2]
    orders = rows - 1
    main = pairs * orders
    used = main + pairs
    chunks = main // 128
    lanes = main + 128
    lat = half_lat // n_ma
    slots = 2 * pairs
    full = n_ma * slots
    points = lon_count(orders)
    bf16 = jnp.bfloat16
    f32 = jnp.float32
    groups = 12 * levels
    scale = (NLON / points) / math.sqrt(NLON) / orders
    angle = np.outer(np.arange(orders), np.arange(points)) % points * (2.0 * math.pi / points)
    table = np.stack([np.cos(angle), -np.sin(angle)])
    tab = jnp.asarray(table, bf16)
    tab_t = jnp.asarray(np.transpose(table, (0, 2, 1)), bf16)
    vmem = pl.BlockSpec(memory_space=pltpu.VMEM)
    smem = pl.BlockSpec(memory_space=pltpu.SMEM)
    out = pl.pallas_call(
        functools.partial(fused_kernel, n_ma, n_row, pairs, rows, levels, scale),
        out_shape=jax.ShapeDtypeStruct((levels, 6, used), f32),
        in_specs=[vmem, vmem, vmem, smem, vmem, smem, vmem, vmem],
        out_specs=vmem,
        scratch_shapes=[
            pltpu.VMEM((n_ma, chunks, lat, 128), bf16),
            pltpu.VMEM((n_ma, 8, 128), bf16),
            pltpu.VMEM((n_ma, chunks, groups, 128), bf16),
            pltpu.VMEM((n_ma, chunks, lat, 128), bf16),
            pltpu.VMEM((n_ma, 8, 128), bf16),
            pltpu.VMEM((128, 128), f32),
            pltpu.VMEM((groups, full, 2 * lat), f32),
            pltpu.VMEM((groups // 2, full, 2 * lat), f32),
            pltpu.VMEM((n_ma, groups // 2, lanes), bf16),
            pltpu.VMEM((n_ma, groups // 2, lanes), bf16),
            pltpu.VMEM((levels + 4, 6, lanes), f32),
        ]
        + [pltpu.SemaphoreType.DMA((n_ma,))] * 10
        + [pltpu.SemaphoreType.DMA((2,))] * 2,
        compiler_params=pltpu.CompilerParams(
            collective_id=0, has_side_effects=True, vmem_limit_bytes=48 * 1024 * 1024
        ),
    )(
        velocity.reshape(6 * levels, pairs, rows),
        vorticity.reshape(6 * levels, pairs, rows),
        jnp.transpose(legendre, (1, 0, 2)),
        pair_order,
        lat_weight,
        diffusivity,
        tab,
        tab_t,
    )
    out = jnp.concatenate(
        [out[..., :main].reshape(levels, 6, pairs, orders), out[..., main:, None]], axis=3
    )
    return jnp.transpose(out.reshape(levels, 3, 2, pairs, rows), (1, 2, 0, 3, 4))


def fits(velocity, legendre):
    n_ma = lax.axis_size("ma")
    n_row = lax.axis_size("row")
    pairs, rows, half_lat = legendre.shape
    levels = velocity.shape[2]
    lat = half_lat // n_ma
    tiles = pairs == 4 and pairs * (rows - 1) == 256 and n_ma % 2 == 0 and n_ma <= 8 and n_row % 2 == 0
    whole = half_lat % n_ma == 0 and lat % 16 == 0 and lat <= 64 and levels == 4
    return tiles and whole and n_row > 2 and n_ma > 1


def step(velocity, vorticity, legendre, pair_order, lat_weight, diffusivity):
    chosen = fused if fits(velocity, legendre) else local
    return chosen(velocity, vorticity, legendre, pair_order, lat_weight, diffusivity)


def solution(mesh):
    in_specs = (
        P(None, None, "row", "ma", None),
        P(None, None, "row", "ma", None),
        P("ma", None, None),
        P("ma"),
        P(),
        P(),
    )
    out_specs = P(None, None, "row", "ma", None)
    return jax.shard_map(step, mesh=mesh, in_specs=in_specs, out_specs=out_specs, check_vma=False)
```
